256 devices in a mesh: ch: 256 (over z, x, y, core).
Axes of the slice: x: 4, y: 4, z: 8, core: 2. Of those that a mesh axis runs over, the one named last changes fastest.
Arguments:
- spectra: bfloat16 [4, 131072, 128], P(None, 'ch'), may hold values from -6 to 6
- offsets: int32 [131072], P('ch'), may hold values from 0 to 7
- bins: int32 [4], replicated, may hold values from 1 to 63
Outputs:
- gradient: float32 [4, 131072, 128], P(None, 'ch')
The draws below stay inside these ranges and needn't reach their ends.
All inputs are finite; a program needn't handle non-finite values.
Results may differ from the reference program's by a relative error of at most 0.0015.
Values may be sent and summed in bfloat16 or wider, within the bound.
A program may use at most 64 MiB of HBM per device.

```python
import math
import jax
import jax.numpy as jnp
from jax import lax

C_DEV = 512
WIN = 64
F = 4
NEXT = 3
NC = 131072
N_CH = 256


def plant(array, own_key, low, high):
    spot = [jax.random.randint(jax.random.fold_in(own_key, axis), (), 0, length) for axis, length in enumerate(array.shape)]
    longest = array.shape.index(max(array.shape))
    neighbour = spot[:longest] + [(spot[longest] + 1) % array.shape[longest]] + spot[longest + 1:]
    return array.at[tuple(spot)].set(low).at[tuple(neighbour)].set(high)


def steps_of(stream_key, shape, split, low, top_value):
    def one(dim, parts):
        draws = jax.random.uniform(jax.random.fold_in(jax.random.fold_in(stream_key, 6), dim), (parts,), jnp.float32, low / len(split), top_value / len(split))
        return jnp.repeat(jnp.exp(draws), shape[dim] // parts).reshape((-1,) + (1,) * (len(shape) - dim - 1))

    gain = one(*split[0])
    for cut in split[1:]:
        gain = gain * one(*cut)
    return gain


def centred(rng, shape, scale, reach, shards=(), kind=jnp.bfloat16):
    loudness = steps_of(rng, shape, shards, -0.22, 0.18) if shards else 1.0
    values = jax.random.normal(rng, shape, jnp.float32) * scale * loudness
    return jnp.minimum(jnp.maximum(values, -reach), reach).astype(kind)


def setup_inputs(seed: int = 0) -> dict:
    key_list = jax.random.split(jax.random.key(seed), 4)
    return {
        "spectra": centred(key_list[0], (F, NC, 2 * WIN), 1.0, 6.0, ((1, 256),)),
        "offsets": plant(jax.random.randint(key_list[1], (NC,), 0, 8), jax.random.fold_in(key_list[1], 1), 0, 7).astype(jnp.int32),
        "bins": plant(jax.random.randint(key_list[2], (F,), 1, 64), jax.random.fold_in(key_list[2], 1), 1, 63).astype(jnp.int32),
    }


spacing_metres = 8
period_metres = 4096
model_amp = 0.5


def block_terms(mine, mine_off, other, other_off, gap, bins):
    windows = mine.shape[2] // 2
    channels = mine.shape[1]
    mine_f = mine.astype(jnp.float32)
    other_f = other.astype(jnp.float32)
    other_swap = jnp.concatenate([-other_f[..., windows:], other_f[..., :windows]], axis=-1)
    mine_swap = jnp.concatenate([mine_f[..., windows:], -mine_f[..., :windows]], axis=-1)
    real_part = jnp.einsum("fik,fjk->fij", mine_f, other_f) / windows
    imag_part = jnp.einsum("fik,fjk->fij", mine_f, other_swap) / windows
    rows = jnp.arange(channels, dtype=jnp.int32)
    distance = (gap + rows[None, :] - rows[:, None]) * spacing_metres + other_off[None, :] - mine_off[:, None]
    wrapped = jnp.mod(bins[:, None, None] * distance[None, :, :], period_metres)
    phase = wrapped.astype(jnp.float32) * (2.0 * math.pi / period_metres)
    grad_real = jnp.tanh(real_part - model_amp * jnp.cos(phase)).astype(jnp.bfloat16).astype(jnp.float32)
    grad_imag = jnp.tanh(imag_part - model_amp * jnp.sin(phase)).astype(jnp.bfloat16).astype(jnp.float32)
    forward_term = jnp.einsum("fij,fjk->fik", grad_real, other_f) + jnp.einsum("fij,fjk->fik", grad_imag, other_swap)
    back_term = jnp.einsum("fij,fik->fjk", grad_real, mine_f) + jnp.einsum("fij,fik->fjk", grad_imag, mine_swap)
    return forward_term, back_term


def reference(spectra, offsets, bins):
    nblocks = N_CH
    channels = C_DEV
    freqs = spectra.shape[0]
    width = spectra.shape[2]
    blocks = spectra.reshape(freqs, nblocks, channels, width).transpose(1, 0, 2, 3)
    blocks = jnp.concatenate([blocks, jnp.zeros((NEXT, freqs, channels, width), blocks.dtype)], axis=0)
    off_blocks = offsets.reshape(nblocks, channels)
    off_blocks = jnp.concatenate([off_blocks, jnp.zeros((NEXT, channels), jnp.int32)], axis=0)

    def one_block(index):
        mine = blocks[index]
        mine_off = off_blocks[index]
        total = jnp.zeros((freqs, channels, width), jnp.float32)
        backs = []
        for distance in range(NEXT + 1):
            other = lax.dynamic_index_in_dim(blocks, (index + distance).astype(jnp.int32), 0, keepdims=False)
            other_off = lax.dynamic_index_in_dim(off_blocks, (index + distance).astype(jnp.int32), 0, keepdims=False)
            forward_term, back_term = block_terms(mine, mine_off, other, other_off, distance * channels, bins)
            total = total + forward_term
            backs.append(back_term)
        return total, jnp.stack(backs)

    forward_all, back_all = lax.map(one_block, jnp.arange(nblocks, dtype=jnp.int32))
    result = forward_all
    for distance in range(NEXT + 1):
        moved = jnp.concatenate([jnp.zeros((distance, freqs, channels, width), jnp.float32), back_all[:, distance]], axis=0)[:nblocks]
        result = result + moved
    result = result / (width // 2)
    return result.transpose(1, 0, 2, 3).reshape(freqs, nblocks * channels, width)
```

```python
import functools
import math

import jax
import jax.numpy as jnp
from jax import lax
from jax.experimental import pallas as pl
from jax.experimental.pallas import tpu as pltpu
from jax.sharding import PartitionSpec as P

spacing_metres = 8
period_metres = 4096
model_amp = 0.5

F32 = jnp.float32
BF16 = jnp.bfloat16
MESH = pl.DeviceIdType.MESH

OWN, PARTNER, M_SAME, P_SAME, M_OTHER, P_OTHER, FAR = range(7)
TO_PARTNER, TO_PLUS, TO_MINUS, FWD_M, FWD_P, FWD_FAR = range(6)


def dot(a, b):
    return lax.dot_general(a, b, (((1,), (0,)), ((), ())), preferred_element_type=F32)


def cos_sin(m):
    quarter = period_metres // 4
    turn = (m + quarter // 2) // quarter
    theta = (m - turn * quarter).astype(F32) * (2.0 * math.pi / period_metres)
    x = theta * theta
    s = theta * (1.0 + x * (-1.0 / 6 + x * (1.0 / 120 + x * (-1.0 / 5040 + x * (1.0 / 362880)))))
    c = 1.0 + x * (-0.5 + x * (1.0 / 24 + x * (-1.0 / 720 + x * (1.0 / 40320))))
    turn = turn & 3
    odd = (turn & 1) == 1
    cos = jnp.where(odd, s, c)
    sin = jnp.where(odd, c, s)
    cos = jnp.where((turn == 1) | (turn == 2), -cos, cos)
    sin = jnp.where(turn >= 2, -sin, sin)
    return cos, sin


def split(v):
    high = v.astype(BF16).astype(F32)
    return high, v - high


def kernel(nfreq, nch, ndev, bins_ref, off_ref, spec_ref, out_ref, blk, aug, wre, wim, acc, offs,
           local_sem, send_sem, recv_sem, off_send, off_recv):
    lanes = 128
    groups = nch // lanes
    me = lax.axis_index("ch")
    nchip = ndev // 2
    chip = me // 2
    core = me - 2 * chip
    up = lax.rem(chip + 1, nchip)
    down = lax.rem(chip + nchip - 1, nchip)
    partner = 2 * chip + (1 - core)
    plus_same, plus_other = 2 * up + core, 2 * up + (1 - core)
    minus_same, minus_other = 2 * down + core, 2 * down + (1 - core)
    far_to = jnp.where(core == 1, plus_other, minus_other)
    far_from = jnp.where(core == 1, M_SAME, P_SAME)

    barrier = pltpu.get_barrier_semaphore()
    for peer in (partner, plus_same, minus_same, plus_other, minus_other):
        pl.semaphore_signal(barrier, inc=1, device_id=(peer,), device_id_type=MESH)

    def own_load(f):
        return pltpu.make_async_copy(spec_ref.at[f], blk.at[OWN, f], local_sem.at[f])

    for f in range(nfreq):
        own_load(f).start()

    aug[...] = jnp.zeros_like(aug)
    wre[:, lanes:, :] = jnp.zeros((nfreq, wre.shape[1] - lanes, nch), BF16)
    wim[:, lanes:, :] = jnp.zeros((nfreq, wim.shape[1] - lanes, nch), BF16)

    def send(kind, f, src, slot, to):
        return pltpu.make_async_remote_copy(
            src_ref=src, dst_ref=blk.at[slot, f], send_sem=send_sem.at[kind, f],
            recv_sem=recv_sem.at[slot, f], device_id=(to,), device_id_type=MESH)

    def sends(f):
        return (
            send(TO_PLUS, f, spec_ref.at[f], M_SAME, plus_same),
            send(TO_MINUS, f, spec_ref.at[f], P_SAME, minus_same),
            send(TO_PARTNER, f, spec_ref.at[f], PARTNER, partner),
        )

    def forwards(f):
        return (
            send(FWD_M, f, blk.at[M_SAME, f], M_OTHER, partner),
            send(FWD_P, f, blk.at[P_SAME, f], P_OTHER, partner),
            send(FWD_FAR, f, blk.at[far_from, f], FAR, far_to),
        )

    def off_copy(n, src, slot, to):
        return pltpu.make_async_remote_copy(
            src_ref=src, dst_ref=offs.at[slot], send_sem=off_send.at[n],
            recv_sem=off_recv.at[slot], device_id=(to,), device_id_type=MESH)

    off_sends = (
        off_copy(0, off_ref, PARTNER, partner),
        off_copy(1, off_ref, M_SAME, plus_same),
        off_copy(2, off_ref, P_SAME, minus_same),
        off_copy(3, off_ref, M_OTHER, plus_other),
        off_copy(4, off_ref, P_OTHER, minus_other),
    )
    off_far = off_copy(5, offs.at[far_from], FAR, far_to)

    def wait_block(slot, f):
        send(TO_PLUS, f, spec_ref.at[f], slot, plus_same).wait_recv()

    row = lax.broadcasted_iota(jnp.int32, (8, lanes), 0)
    part = row & 3

    def pick(parts, a, b, c, d):
        return jnp.where(parts == 0, a, jnp.where(parts == 1, b, jnp.where(parts == 2, c, d)))

    def tables(off):
        shape = off.shape
        place = lax.broadcasted_iota(jnp.int32, shape, 1) * lanes + lax.broadcasted_iota(jnp.int32, shape, 2)
        pos = place * spacing_metres + off
        result = []
        for f in range(nfreq):
            cos, sin = cos_sin((bins_ref[f] * pos) & (period_metres - 1))
            result.append(split(cos) + split(sin))
        return result

    def put_aug(slot, table, n):
        for g in range(groups):
            rows = []
            for f in range(nfreq):
                ch, cl, sh, sl = (v[n, g : g + 1, :] for v in table[f])
                rows.append(pick(part, ch, cl, sh, sl))
            block = jnp.concatenate(rows, axis=0)
            aug[slot, g * lanes : (g + 1) * lanes, 0 : 8 * nfreq] = block.T.astype(BF16)

    own_table = tables(off_ref[...].reshape(1, groups, lanes))
    put_aug(OWN, own_table, 0)
    late = row >= 4
    cosine = part < 2
    nothing = jnp.zeros((8, lanes), F32)
    for g in range(groups):
        for f in range(nfreq):
            ch, cl, sh, sl = (v[0, g : g + 1, :] for v in own_table[f])
            cos = jnp.where(late, cl, ch)
            sin = jnp.where(late, sl, sh)
            real = jnp.where(cosine, cos, sin) * (-model_amp)
            imag = jnp.where(cosine, sin, -cos) * model_amp
            cols = slice(g * lanes, (g + 1) * lanes)
            rows = slice(lanes, lanes + 8 * nfreq)
            wre[f, rows, cols] = jnp.concatenate(
                [real if n == f else nothing for n in range(nfreq)], axis=0).astype(BF16)
            wim[f, rows, cols] = jnp.concatenate(
                [imag if n == f else nothing for n in range(nfreq)], axis=0).astype(BF16)

    pl.semaphore_wait(barrier, 5)
    for copy in off_sends:
        copy.start()
    for f in range(nfreq):
        for copy in sends(f):
            copy.start()

    half = lanes // 2
    scale = 1.0 / half

    def transposed(slot, f):
        t = blk[slot, f].T
        return t, jnp.concatenate([-t[half:], t[:half]], axis=0)

    def grads(slot, f):
        x = jnp.concatenate([blk[slot, f], aug[slot]], axis=1)
        real = jnp.tanh(dot(x, wre[f])).astype(BF16)
        imag = jnp.tanh(dot(x, wim[f])).astype(BF16)
        return real, imag

    def terms(slot, f, g):
        t, swapped = transposed(slot, f)
        return dot(t, g[0]) + dot(swapped, g[1])

    def own_step(i, carry):
        fs = [2 * i, 2 * i + 1]
        for f in fs:
            own_load(f).wait()
            t, swapped = transposed(OWN, f)
            wre[f, :lanes, :] = t * jnp.array(scale, BF16)
            wim[f, :lanes, :] = swapped * jnp.array(-scale, BF16)
        g = [grads(OWN, f) for f in fs]
        for f, v in zip(fs, g):
            acc[f] = 2.0 * terms(OWN, f, v)
        return carry

    lax.fori_loop(0, nfreq // 2, own_step, 0)

    for slot in (PARTNER, M_SAME, P_SAME, M_OTHER, P_OTHER):
        off_copy(0, off_ref, slot, partner).wait_recv()
    off_far.start()
    table = tables(offs[PARTNER : P_OTHER + 1])
    for slot in range(PARTNER, P_OTHER + 1):
        put_aug(slot, table, slot - PARTNER)

    def partner_step(i, carry):
        fs = [2 * i, 2 * i + 1]
        for f in fs:
            wait_block(PARTNER, f)
        g = [grads(PARTNER, f) for f in fs]
        for f, v in zip(fs, g):
            acc[f] += terms(PARTNER, f, v)
        return carry

    lax.fori_loop(0, nfreq // 2, partner_step, 0)

    has_m = jnp.where(chip >= 1, 1.0, 0.0).astype(F32)
    has_p = jnp.where(chip < nchip - 1, 1.0, 0.0).astype(F32)
    has_far = jnp.where(core == 1, chip < nchip - 2, chip >= 2)
    has_far = jnp.where(has_far, 1.0, 0.0).astype(F32)

    def pair(m_slot, p_slot, f):
        gm = grads(m_slot, f)
        gp = grads(p_slot, f)
        acc[f] += has_m * terms(m_slot, f, gm) + has_p * terms(p_slot, f, gp)

    def near_step(f, carry):
        wait_block(M_SAME, f)
        wait_block(P_SAME, f)
        for copy in forwards(f):
            copy.start()
        pair(M_SAME, P_SAME, f)
        wait_block(M_OTHER, f)
        wait_block(P_OTHER, f)
        pair(M_OTHER, P_OTHER, f)
        return carry

    lax.fori_loop(0, nfreq, near_step, 0)

    off_copy(0, off_ref, FAR, partner).wait_recv()
    put_aug(FAR, tables(offs[FAR : FAR + 1]), 0)

    def far_step(f, carry):
        wait_block(FAR, f)
        total = acc[f] + has_far * terms(FAR, f, grads(FAR, f))
        out_ref[f] = total.T * scale
        return carry

    lax.fori_loop(0, nfreq, far_step, 0)

    for copy in off_sends + (off_far,):
        copy.wait_send()
    for f in range(nfreq):
        for copy in sends(f) + forwards(f):
            copy.wait_send()


def local(ndev, spectra, offsets, bins):
    nfreq, nch, width = spectra.shape
    lanes = 128
    assert width == lanes and nch % lanes == 0 and nfreq % 2 == 0 and 8 * nfreq <= lanes
    assert (nch * spacing_metres) % period_metres == 0
    vmem = pl.BlockSpec(memory_space=pltpu.VMEM)
    return pl.pallas_call(
        functools.partial(kernel, nfreq, nch, ndev),
        out_shape=jax.ShapeDtypeStruct((nfreq, nch, width), F32),
        in_specs=[pl.BlockSpec(memory_space=pltpu.SMEM), vmem, pl.BlockSpec(memory_space=pl.ANY)],
        out_specs=vmem,
        scratch_shapes=[
            pltpu.VMEM((7, nfreq, nch, width), BF16),
            pltpu.VMEM((7, nch, lanes), BF16),
            pltpu.VMEM((nfreq, 2 * lanes, nch), BF16),
            pltpu.VMEM((nfreq, 2 * lanes, nch), BF16),
            pltpu.VMEM((nfreq, width, nch), F32),
            pltpu.VMEM((7, nch // lanes, lanes), jnp.int32),
            pltpu.SemaphoreType.DMA((nfreq,)),
            pltpu.SemaphoreType.DMA((6, nfreq)),
            pltpu.SemaphoreType.DMA((7, nfreq)),
            pltpu.SemaphoreType.DMA((6,)),
            pltpu.SemaphoreType.DMA((7,)),
        ],
        compiler_params=pltpu.CompilerParams(
            collective_id=0, has_side_effects=True, vmem_limit_bytes=56 << 20),
    )(bins, offsets.reshape(nch // lanes, lanes), spectra)


def solution(mesh):
    return jax.shard_map(
        functools.partial(local, mesh.shape["ch"]),
        mesh=mesh,
        in_specs=(P(None, "ch", None), P("ch"), P()),
        out_specs=P(None, "ch", None),
        check_vma=False,
    )
```

```python
import functools
import math

import jax
import jax.numpy as jnp
from jax import lax
from jax.experimental import pallas as pl
from jax.experimental.pallas import tpu as pltpu
from jax.sharding import PartitionSpec as P

spacing_metres = 8
period_metres = 4096
model_amp = 0.5

F32 = jnp.float32
BF16 = jnp.bfloat16
MESH = pl.DeviceIdType.MESH

OWN, PARTNER, M_SAME, P_SAME, M_OTHER, P_OTHER, FAR = range(7)
TO_PARTNER, TO_PLUS, TO_MINUS, FWD_M, FWD_P, FWD_FAR = range(6)


def dot(a, b):
    return lax.dot_general(a, b, (((1,), (0,)), ((), ())), preferred_element_type=F32)


def cos_sin(m):
    quarter = period_metres // 4
    turn = (m + quarter // 2) // quarter
    theta = (m - turn * quarter).astype(F32) * (2.0 * math.pi / period_metres)
    x = theta * theta
    s = theta * (1.0 + x * (-1.0 / 6 + x * (1.0 / 120 + x * (-1.0 / 5040 + x * (1.0 / 362880)))))
    c = 1.0 + x * (-0.5 + x * (1.0 / 24 + x * (-1.0 / 720 + x * (1.0 / 40320))))
    turn = turn & 3
    odd = (turn & 1) == 1
    cos = jnp.where(odd, s, c)
    sin = jnp.where(odd, c, s)
    cos = jnp.where((turn == 1) | (turn == 2), -cos, cos)
    sin = jnp.where(turn >= 2, -sin, sin)
    return cos, sin


def split(v):
    high = v.astype(BF16).astype(F32)
    return high, v - high


def kernel(nfreq, nch, ndev, bins_hbm, off_ref, spec_ref, out_ref, blk, aug, wre, wim, acc, res, offs, bins_ref,
           in_sem, local_sem, out_sem, send_sem, recv_sem, off_send, off_recv):
    lanes = 128
    groups = nch // lanes
    me = lax.axis_index("ch")
    nchip = ndev // 2
    chip = me // 2
    core = me - 2 * chip
    up = jnp.minimum(chip + 1, nchip - 1)
    down = jnp.maximum(chip - 1, 0)
    has_up = chip < nchip - 1
    has_down = chip >= 1
    partner = 2 * chip + (1 - core)
    plus_same, plus_other = 2 * up + core, 2 * up + (1 - core)
    minus_same, minus_other = 2 * down + core, 2 * down + (1 - core)
    upward = core == 1
    far_to = jnp.where(upward, plus_other, minus_other)
    far_from = jnp.where(upward, M_SAME, P_SAME)
    sends_far = has_up & has_down
    has_far = jnp.where(upward, chip < nchip - 2, chip >= 2)

    barrier = pltpu.get_barrier_semaphore()

    def greet(peer):
        pl.semaphore_signal(barrier, inc=1, device_id=(peer,), device_id_type=MESH)

    @pl.when(has_up)
    def _():
        greet(plus_same)
        greet(plus_other)

    @pl.when(has_down)
    def _():
        greet(minus_same)
        greet(minus_other)

    greet(partner)

    def own_load(f):
        return pltpu.make_async_copy(spec_ref.at[f], blk.at[OWN, f], local_sem.at[f])

    bins_load = pltpu.make_async_copy(bins_hbm, bins_ref, in_sem.at[0])
    off_load = pltpu.make_async_copy(off_ref, offs.at[OWN], in_sem.at[1])
    bins_load.start()
    off_load.start()
    for f in range(nfreq):
        own_load(f).start()

    def clear(slots, freqs):
        for slot in slots:
            offs[slot] = jnp.zeros(offs.shape[1:], offs.dtype)
            for f in range(freqs):
                blk[slot, f] = jnp.zeros(blk.shape[2:], blk.dtype)

    @pl.when(jnp.logical_not(has_down))
    def _():
        clear((M_SAME, M_OTHER), nfreq)

    @pl.when(jnp.logical_not(has_up))
    def _():
        clear((P_SAME, P_OTHER), nfreq)

    @pl.when(jnp.logical_not(has_far))
    def _():
        clear((FAR,), nfreq)

    aug[...] = jnp.zeros_like(aug)
    wre[:, lanes:, :] = jnp.zeros((nfreq, wre.shape[1] - lanes, nch), BF16)
    wim[:, lanes:, :] = jnp.zeros((nfreq, wim.shape[1] - lanes, nch), BF16)

    def send(kind, f, src, slot, to):
        return pltpu.make_async_remote_copy(
            src_ref=src, dst_ref=blk.at[slot, f], send_sem=send_sem.at[kind, f],
            recv_sem=recv_sem.at[slot, f], device_id=(to,), device_id_type=MESH)

    def to_plus(f):
        return send(TO_PLUS, f, spec_ref.at[f], M_SAME, plus_same)

    def to_minus(f):
        return send(TO_MINUS, f, spec_ref.at[f], P_SAME, minus_same)

    def to_partner(f):
        return send(TO_PARTNER, f, spec_ref.at[f], PARTNER, partner)

    def forward_m(f):
        return send(FWD_M, f, blk.at[M_SAME, f], M_OTHER, partner)

    def forward_p(f):
        return send(FWD_P, f, blk.at[P_SAME, f], P_OTHER, partner)

    def forward_far(f):
        return send(FWD_FAR, f, blk.at[far_from, f], FAR, far_to)

    def off_copy(n, src, slot, to):
        return pltpu.make_async_remote_copy(
            src_ref=src, dst_ref=offs.at[slot], send_sem=off_send.at[n],
            recv_sem=off_recv.at[slot], device_id=(to,), device_id_type=MESH)

    off_partner = off_copy(0, off_ref, PARTNER, partner)
    off_up = (off_copy(1, off_ref, M_SAME, plus_same), off_copy(3, off_ref, M_OTHER, plus_other))
    off_down = (off_copy(2, off_ref, P_SAME, minus_same), off_copy(4, off_ref, P_OTHER, minus_other))
    off_far = off_copy(5, offs.at[far_from], FAR, far_to)

    def wait_block(slot, f):
        send(TO_PLUS, f, spec_ref.at[f], slot, partner).wait_recv()

    def wait_offsets(slot):
        off_copy(0, off_ref, slot, partner).wait_recv()

    row = lax.broadcasted_iota(jnp.int32, (8, lanes), 0)
    part = row & 3

    def pick(parts, a, b, c, d):
        return jnp.where(parts == 0, a, jnp.where(parts == 1, b, jnp.where(parts == 2, c, d)))

    def tables(off):
        shape = off.shape
        place = lax.broadcasted_iota(jnp.int32, shape, 1) * lanes + lax.broadcasted_iota(jnp.int32, shape, 2)
        pos = place * spacing_metres + off
        result = []
        for f in range(nfreq):
            cos, sin = cos_sin((bins_ref[f] * pos) & (period_metres - 1))
            result.append(split(cos) + split(sin))
        return result

    def put_aug(slot, table, n):
        for g in range(groups):
            rows = []
            for f in range(nfreq):
                ch, cl, sh, sl = (v[n, g : g + 1, :] for v in table[f])
                rows.append(pick(part, ch, cl, sh, sl))
            block = jnp.concatenate(rows, axis=0)
            aug[slot, g * lanes : (g + 1) * lanes, 0 : 8 * nfreq] = block.T.astype(BF16)

    bins_load.wait()
    off_load.wait()
    own_table = tables(offs[OWN : OWN + 1])
    put_aug(OWN, own_table, 0)
    late = row >= 4
    cosine = part < 2
    nothing = jnp.zeros((8, lanes), F32)
    for g in range(groups):
        for f in range(nfreq):
            ch, cl, sh, sl = (v[0, g : g + 1, :] for v in own_table[f])
            cos = jnp.where(late, cl, ch)
            sin = jnp.where(late, sl, sh)
            real = jnp.where(cosine, cos, sin) * (-model_amp)
            imag = jnp.where(cosine, sin, -cos) * model_amp
            cols = slice(g * lanes, (g + 1) * lanes)
            rows = slice(lanes, lanes + 8 * nfreq)
            wre[f, rows, cols] = jnp.concatenate(
                [real if n == f else nothing for n in range(nfreq)], axis=0).astype(BF16)
            wim[f, rows, cols] = jnp.concatenate(
                [imag if n == f else nothing for n in range(nfreq)], axis=0).astype(BF16)

    greeted = 1 + 2 * has_up.astype(jnp.int32) + 2 * has_down.astype(jnp.int32)
    pl.semaphore_wait(barrier, greeted)

    @pl.when(has_up)
    def _():
        for copy in off_up:
            copy.start()
        to_plus(0).start()

    @pl.when(has_down)
    def _():
        for copy in off_down:
            copy.start()
        to_minus(0).start()

    off_partner.start()
    to_partner(0).start()
    for f in range(1, nfreq):
        pl.when(has_up)(lambda f=f: to_plus(f).start())
        pl.when(has_down)(lambda f=f: to_minus(f).start())
        to_partner(f).start()

    half = lanes // 2
    scale = 1.0 / half

    def transposed(slot, f):
        t = blk[slot, f].T
        return t, jnp.concatenate([-t[half:], t[:half]], axis=0)

    def grads(slot, f):
        x = jnp.concatenate([blk[slot, f], aug[slot]], axis=1)
        real = jnp.tanh(dot(x, wre[f])).astype(BF16)
        imag = jnp.tanh(dot(x, wim[f])).astype(BF16)
        return real, imag

    def terms(slot, f, g):
        t, swapped = transposed(slot, f)
        return dot(t, g[0]) + dot(swapped, g[1])

    def own_step(i, carry):
        fs = [2 * i, 2 * i + 1]
        for f in fs:
            own_load(f).wait()
            t, swapped = transposed(OWN, f)
            wre[f, :lanes, :] = t * jnp.array(scale, BF16)
            wim[f, :lanes, :] = swapped * jnp.array(-scale, BF16)
        g = [grads(OWN, f) for f in fs]
        for f, v in zip(fs, g):
            acc[f] = 2.0 * terms(OWN, f, v)
        return carry

    lax.fori_loop(0, nfreq // 2, own_step, 0)

    wait_offsets(PARTNER)

    @pl.when(has_down)
    def _():
        wait_offsets(M_SAME)
        wait_offsets(M_OTHER)

    @pl.when(has_up)
    def _():
        wait_offsets(P_SAME)
        wait_offsets(P_OTHER)

    @pl.when(sends_far)
    def _():
        off_far.start()

    table = tables(offs[PARTNER : P_OTHER + 1])
    for slot in range(PARTNER, P_OTHER + 1):
        put_aug(slot, table, slot - PARTNER)

    def partner_step(i, carry):
        fs = [2 * i, 2 * i + 1]
        for f in fs:
            wait_block(PARTNER, f)
        g = [grads(PARTNER, f) for f in fs]
        for f, v in zip(fs, g):
            acc[f] += terms(PARTNER, f, v)
        return carry

    lax.fori_loop(0, nfreq // 2, partner_step, 0)

    def pair(m_slot, p_slot, f):
        gm = grads(m_slot, f)
        gp = grads(p_slot, f)
        acc[f] += terms(m_slot, f, gm) + terms(p_slot, f, gp)

    def near_step(f, carry):
        @pl.when(f == nfreq - 1)
        def _():
            pl.when(has_far)(lambda: wait_offsets(FAR))
            put_aug(FAR, tables(offs[FAR : FAR + 1]), 0)

        @pl.when(has_down)
        def _():
            wait_block(M_SAME, f)
            forward_m(f).start()

        @pl.when(has_up)
        def _():
            wait_block(P_SAME, f)
            forward_p(f).start()

        @pl.when(sends_far)
        def _():
            forward_far(f).start()

        pair(M_SAME, P_SAME, f)
        pl.when(has_down)(lambda: wait_block(M_OTHER, f))
        pl.when(has_up)(lambda: wait_block(P_OTHER, f))
        pair(M_OTHER, P_OTHER, f)
        return carry

    lax.fori_loop(0, nfreq, near_step, 0)

    def store(f):
        return pltpu.make_async_copy(res.at[f], out_ref.at[f], out_sem.at[f])

    def far_step(f, carry):
        pl.when(has_far)(lambda: wait_block(FAR, f))
        total = acc[f] + terms(FAR, f, grads(FAR, f))
        res[f] = total.T * scale
        store(f).start()
        return carry

    lax.fori_loop(0, nfreq, far_step, 0)

    off_partner.wait_send()

    @pl.when(has_up)
    def _():
        for copy in off_up:
            copy.wait_send()

    @pl.when(has_down)
    def _():
        for copy in off_down:
            copy.wait_send()

    pl.when(sends_far)(lambda: off_far.wait_send())
    for f in range(nfreq):
        to_partner(f).wait_send()

        @pl.when(has_up)
        def _():
            to_plus(f).wait_send()
            forward_p(f).wait_send()

        @pl.when(has_down)
        def _():
            to_minus(f).wait_send()
            forward_m(f).wait_send()

        pl.when(sends_far)(lambda: forward_far(f).wait_send())
    for f in range(nfreq):
        store(f).wait()


def local(ndev, spectra, offsets, bins):
    nfreq, nch, width = spectra.shape
    lanes = 128
    assert width == lanes and nch % lanes == 0 and nfreq % 2 == 0 and 8 * nfreq <= lanes
    assert (nch * spacing_metres) % period_metres == 0
    hbm = pl.BlockSpec(memory_space=pltpu.HBM)
    args = (bins, offsets.reshape(nch // lanes, lanes), spectra)
    return pl.pallas_call(
        functools.partial(kernel, nfreq, nch, ndev),
        out_shape=jax.ShapeDtypeStruct((nfreq, nch, width), F32),
        in_specs=[hbm, hbm, hbm],
        out_specs=pl.BlockSpec(memory_space=pl.ANY),
        scratch_shapes=[
            pltpu.VMEM((7, nfreq, nch, width), BF16),
            pltpu.VMEM((7, nch, lanes), BF16),
            pltpu.VMEM((nfreq, 2 * lanes, nch), BF16),
            pltpu.VMEM((nfreq, 2 * lanes, nch), BF16),
            pltpu.VMEM((nfreq, width, nch), F32),
            pltpu.VMEM((nfreq, nch, width), F32),
            pltpu.VMEM((7, nch // lanes, lanes), jnp.int32),
            pltpu.SMEM((nfreq,), jnp.int32),
            pltpu.SemaphoreType.DMA((2,)),
            pltpu.SemaphoreType.DMA((nfreq,)),
            pltpu.SemaphoreType.DMA((nfreq,)),
            pltpu.SemaphoreType.DMA((6, nfreq)),
            pltpu.SemaphoreType.DMA((7, nfreq)),
            pltpu.SemaphoreType.DMA((6,)),
            pltpu.SemaphoreType.DMA((7,)),
        ],
        compiler_params=pltpu.CompilerParams(
            collective_id=0, has_side_effects=True, vmem_limit_bytes=24 << 20),
    )(*(pltpu.with_memory_space_constraint(v, pltpu.HBM) for v in args))


def solution(mesh):
    return jax.shard_map(
        functools.partial(local, mesh.shape["ch"]),
        mesh=mesh,
        in_specs=(P(None, "ch", None), P("ch"), P()),
        out_specs=P(None, "ch", None),
        check_vma=False,
    )
```

```python
import functools
import math

import jax
import jax.numpy as jnp
from jax import lax
from jax.experimental import pallas as pl
from jax.experimental.pallas import tpu as pltpu
from jax.sharding import PartitionSpec as P

spacing_metres = 8
period_metres = 4096
model_amp = 0.5

F32 = jnp.float32
BF16 = jnp.bfloat16
MESH = pl.DeviceIdType.MESH

OWN, PARTNER, M_SAME, P_SAME, M_OTHER, P_OTHER, FAR = range(7)
TO_PARTNER, TO_PLUS, TO_MINUS, FWD_M, FWD_P, FWD_FAR, DETOUR = range(7)

PLANE = 16
DETOURS = 1

EVEN = sum(([(M_SAME, f), (P_SAME, f), (M_OTHER, f), (P_OTHER, f)] for f in range(4)), [])
EVEN = EVEN + [(FAR, f) for f in range(4)]


def lopsided(early, early_other, late, late_other):
    start = [
        (early, 0), (early, 1), (early_other, 0), (early_other, 1), (early, 2), (late, 0), (early_other, 2),
        (late_other, 0), (early, 3), (late, 1), (early_other, 3), (late_other, 1)]
    return start + [
        (late, 2), (late_other, 2), (late, 3), (FAR, 0), (late_other, 3), (FAR, 1), (FAR, 2), (FAR, 3)]


ORDERS = (EVEN, lopsided(P_SAME, P_OTHER, M_SAME, M_OTHER), lopsided(M_SAME, M_OTHER, P_SAME, P_OTHER))


def packed(values, bits):
    return sum(v << (bits * i) for i, v in enumerate(values))


def dot(a, b):
    return lax.dot_general(a, b, (((1,), (0,)), ((), ())), preferred_element_type=F32)


def cos_sin(m):
    quarter = period_metres // 4
    turn = (m + quarter // 2) // quarter
    theta = (m - turn * quarter).astype(F32) * (2.0 * math.pi / period_metres)
    x = theta * theta
    s = theta * (1.0 + x * (-1.0 / 6 + x * (1.0 / 120 + x * (-1.0 / 5040 + x * (1.0 / 362880)))))
    c = 1.0 + x * (-0.5 + x * (1.0 / 24 + x * (-1.0 / 720 + x * (1.0 / 40320))))
    turn = turn & 3
    odd = (turn & 1) == 1
    cos = jnp.where(odd, s, c)
    sin = jnp.where(odd, c, s)
    cos = jnp.where((turn == 1) | (turn == 2), -cos, cos)
    sin = jnp.where(turn >= 2, -sin, sin)
    return cos, sin


def split(v):
    high = v.astype(BF16).astype(F32)
    return high, v - high


def kernel(nfreq, nch, ndev, bins_hbm, off_ref, spec_ref, out_ref, blk, aug, wre, wim, acc, offs, bins_ref,
           in_sem, local_sem, send_sem, recv_sem, off_send, off_recv, via, via_off, via_recv):
    lanes = 128
    groups = nch // lanes
    me = lax.axis_index("ch")
    nchip = ndev // 2
    chip = me // 2
    core = me - 2 * chip
    up = jnp.minimum(chip + 1, nchip - 1)
    down = jnp.maximum(chip - 1, 0)
    has_up = chip < nchip - 1
    has_down = chip >= 1
    partner = 2 * chip + (1 - core)
    plus_same, plus_other = 2 * up + core, 2 * up + (1 - core)
    minus_same, minus_other = 2 * down + core, 2 * down + (1 - core)
    upward = core == 1
    far_to = jnp.where(upward, plus_other, minus_other)
    far_from = jnp.where(upward, M_SAME, P_SAME)
    sends_far = has_up & has_down
    has_far = jnp.where(upward, chip < nchip - 2, chip >= 2)
    def stepped(place):
        return lax.rem(place + PLANE, PLANE) == 0

    spared = sends_far & jnp.where(upward, stepped(chip + 1), stepped(chip))
    detours = jnp.where(upward, stepped(chip + 3) & (chip + 4 < nchip), stepped(chip - 2) & (chip >= 4))
    relays = jnp.where(upward, stepped(chip - 1) & (chip >= 4), stepped(chip + 2) & (chip + 4 < nchip))
    four_up, four_down = 2 * jnp.minimum(chip + 4, nchip - 1) + core, 2 * jnp.maximum(chip - 4, 0) + core
    detour_to = jnp.where(upward, four_up, four_down)
    detour_from = jnp.where(upward, P_SAME, M_SAME)
    relay_from = jnp.where(upward, four_down, four_up)
    relay_to = jnp.where(upward, minus_other, plus_other)
    late_m = (lax.rem(chip, PLANE) == 0) & has_down
    late_p = (lax.rem(chip + 1, PLANE) == 0) & has_up
    edge = late_m | late_p

    def coded(first, field, bits):
        even, m, p = (packed([unit[field] for unit in order[first::2]], bits) for order in ORDERS)
        return jnp.where(late_m, m, jnp.where(late_p, p, even))

    codes = [(coded(n, 0, 3), coded(n, 1, 2)) for n in range(2)]

    barrier = pltpu.get_barrier_semaphore()

    def greet(peer):
        pl.semaphore_signal(barrier, inc=1, device_id=(peer,), device_id_type=MESH)

    @pl.when(has_up)
    def _():
        greet(plus_same)
        greet(plus_other)

    @pl.when(has_down)
    def _():
        greet(minus_same)
        greet(minus_other)

    greet(partner)
    pl.when(detours)(lambda: greet(detour_to))
    pl.when(relays)(lambda: greet(relay_from))

    def own_load(f):
        return pltpu.make_async_copy(spec_ref.at[f], blk.at[OWN, f], local_sem.at[f])

    bins_load = pltpu.make_async_copy(bins_hbm, bins_ref, in_sem.at[0])
    off_load = pltpu.make_async_copy(off_ref, offs.at[OWN], in_sem.at[1])
    bins_load.start()
    off_load.start()
    for f in range(nfreq):
        own_load(f).start()

    def clear(slots, freqs):
        for slot in slots:
            offs[slot] = jnp.zeros(offs.shape[1:], offs.dtype)
            for f in range(freqs):
                blk[slot, f] = jnp.zeros(blk.shape[2:], blk.dtype)

    @pl.when(jnp.logical_not(has_down))
    def _():
        clear((M_SAME, M_OTHER), nfreq)

    @pl.when(jnp.logical_not(has_up))
    def _():
        clear((P_SAME, P_OTHER), nfreq)

    @pl.when(jnp.logical_not(has_far))
    def _():
        clear((FAR,), nfreq)

    aug[...] = jnp.zeros_like(aug)
    wre[:, lanes:, :] = jnp.zeros((nfreq, wre.shape[1] - lanes, nch), BF16)
    wim[:, lanes:, :] = jnp.zeros((nfreq, wim.shape[1] - lanes, nch), BF16)

    def send(kind, f, src, slot, to):
        return pltpu.make_async_remote_copy(
            src_ref=src, dst_ref=blk.at[slot, f], send_sem=send_sem.at[kind, f],
            recv_sem=recv_sem.at[slot, f], device_id=(to,), device_id_type=MESH)

    def to_plus(f):
        return send(TO_PLUS, f, spec_ref.at[f], M_SAME, plus_same)

    def to_minus(f):
        return send(TO_MINUS, f, spec_ref.at[f], P_SAME, minus_same)

    def to_partner(f):
        return send(TO_PARTNER, f, spec_ref.at[f], PARTNER, partner)

    def forward(slot, f):
        return send(slot + FWD_M - M_SAME, f, blk.at[slot, f], slot + M_OTHER - M_SAME, partner)

    def forward_far(f):
        return send(FWD_FAR, f, blk.at[far_from, f], FAR, far_to)

    def detour(f):
        return pltpu.make_async_remote_copy(
            src_ref=blk.at[detour_from, f], dst_ref=via.at[f], send_sem=send_sem.at[DETOUR, f],
            recv_sem=via_recv.at[f], device_id=(detour_to,), device_id_type=MESH)

    def relay(f):
        return send(DETOUR, f, via.at[f], FAR, relay_to)

    def off_copy(n, src, slot, to):
        return pltpu.make_async_remote_copy(
            src_ref=src, dst_ref=offs.at[slot], send_sem=off_send.at[n],
            recv_sem=off_recv.at[slot], device_id=(to,), device_id_type=MESH)

    off_partner = off_copy(0, off_ref, PARTNER, partner)
    off_up = (off_copy(1, off_ref, M_SAME, plus_same), off_copy(3, off_ref, M_OTHER, plus_other))
    off_down = (off_copy(2, off_ref, P_SAME, minus_same), off_copy(4, off_ref, P_OTHER, minus_other))
    off_far = off_copy(5, offs.at[far_from], FAR, far_to)
    off_detour = pltpu.make_async_remote_copy(
        src_ref=offs.at[detour_from], dst_ref=via_off, send_sem=off_send.at[6],
        recv_sem=via_recv.at[DETOURS], device_id=(detour_to,), device_id_type=MESH)
    off_relay = off_copy(6, via_off, FAR, relay_to)

    def wait_block(slot, f):
        send(TO_PLUS, f, spec_ref.at[f], slot, partner).wait_recv()

    def wait_offsets(slot):
        off_copy(0, off_ref, slot, partner).wait_recv()

    row = lax.broadcasted_iota(jnp.int32, (8, lanes), 0)
    part = row & 3

    def pick(parts, a, b, c, d):
        return jnp.where(parts == 0, a, jnp.where(parts == 1, b, jnp.where(parts == 2, c, d)))

    def tables(off):
        shape = off.shape
        place = lax.broadcasted_iota(jnp.int32, shape, 1) * lanes + lax.broadcasted_iota(jnp.int32, shape, 2)
        pos = place * spacing_metres + off
        result = []
        for f in range(nfreq):
            cos, sin = cos_sin((bins_ref[f] * pos) & (period_metres - 1))
            result.append(split(cos) + split(sin))
        return result

    def put_aug(slot, table, n):
        for g in range(groups):
            rows = []
            for f in range(nfreq):
                ch, cl, sh, sl = (v[n, g : g + 1, :] for v in table[f])
                rows.append(pick(part, ch, cl, sh, sl))
            block = jnp.concatenate(rows, axis=0)
            aug[slot, g * lanes : (g + 1) * lanes, 0 : 8 * nfreq] = block.T.astype(BF16)

    bins_load.wait()
    off_load.wait()
    own_table = tables(offs[OWN : OWN + 1])
    put_aug(OWN, own_table, 0)
    late = row >= 4
    cosine = part < 2
    nothing = jnp.zeros((8, lanes), F32)
    for g in range(groups):
        for f in range(nfreq):
            ch, cl, sh, sl = (v[0, g : g + 1, :] for v in own_table[f])
            cos = jnp.where(late, cl, ch)
            sin = jnp.where(late, sl, sh)
            real = jnp.where(cosine, cos, sin) * (-model_amp)
            imag = jnp.where(cosine, sin, -cos) * model_amp
            cols = slice(g * lanes, (g + 1) * lanes)
            rows = slice(lanes, lanes + 8 * nfreq)
            wre[f, rows, cols] = jnp.concatenate(
                [real if n == f else nothing for n in range(nfreq)], axis=0).astype(BF16)
            wim[f, rows, cols] = jnp.concatenate(
                [imag if n == f else nothing for n in range(nfreq)], axis=0).astype(BF16)

    def open_links():
        greeted = 1 + 2 * has_up.astype(jnp.int32) + 2 * has_down.astype(jnp.int32)
        greeted += (detours | relays).astype(jnp.int32)
        pl.semaphore_wait(barrier, greeted)

        @pl.when(has_up)
        def _():
            for copy in off_up:
                copy.start()
            to_plus(0).start()

        @pl.when(has_down)
        def _():
            for copy in off_down:
                copy.start()
            to_minus(0).start()

        off_partner.start()
        to_partner(0).start()
        for f in range(1, nfreq):
            pl.when(has_up)(lambda f=f: to_plus(f).start())
            pl.when(has_down)(lambda f=f: to_minus(f).start())
            to_partner(f).start()

    pl.when(jnp.logical_not(edge))(open_links)

    half = lanes // 2
    scale = 1.0 / half

    def transposed(slot, f):
        t = blk[slot, f].T
        return t, jnp.concatenate([-t[half:], t[:half]], axis=0)

    def grads(slot, f):
        x = jnp.concatenate([blk[slot, f], aug[slot]], axis=1)
        real = jnp.tanh(dot(x, wre[f])).astype(BF16)
        imag = jnp.tanh(dot(x, wim[f])).astype(BF16)
        return real, imag

    def terms(slot, f, g):
        t, swapped = transposed(slot, f)
        return dot(t, g[0]) + dot(swapped, g[1])

    def own_step(i, carry):
        fs = [2 * i, 2 * i + 1]
        for f in fs:
            own_load(f).wait()
            t, swapped = transposed(OWN, f)
            wre[f, :lanes, :] = t * jnp.array(scale, BF16)
            wim[f, :lanes, :] = swapped * jnp.array(-scale, BF16)
        g = [grads(OWN, f) for f in fs]
        for f, v in zip(fs, g):
            acc[f] = 2.0 * terms(OWN, f, v)
        return carry

    lax.fori_loop(0, nfreq // 2, own_step, 0)
    pl.when(edge)(open_links)

    wait_offsets(PARTNER)
    put_aug(PARTNER, tables(offs[PARTNER : PARTNER + 1]), 0)

    def partner_step(i, carry):
        fs = [2 * i, 2 * i + 1]
        for f in fs:
            wait_block(PARTNER, f)
        g = [grads(PARTNER, f) for f in fs]
        for f, v in zip(fs, g):
            acc[f] += terms(PARTNER, f, v)
        return carry

    lax.fori_loop(0, nfreq // 2, partner_step, 0)

    @pl.when(has_down)
    def _():
        wait_offsets(M_SAME)
        wait_offsets(M_OTHER)

    @pl.when(has_up)
    def _():
        wait_offsets(P_SAME)
        wait_offsets(P_OTHER)

    @pl.when(sends_far & jnp.logical_not(spared))
    def _():
        off_far.start()

    pl.when(detours)(lambda: off_detour.start())

    table = tables(offs[M_SAME : P_OTHER + 1])
    for slot in range(M_SAME, P_OTHER + 1):
        put_aug(slot, table, slot - M_SAME)

    def arrive(slot, f):
        there = jnp.where(slot == FAR, has_far, jnp.where((slot & 1) == 1, has_up, has_down))

        @pl.when(there)
        def _():
            wait_block(slot, f)

        @pl.when(there & (slot <= P_SAME))
        def _():
            forward(slot, f).start()

        @pl.when(sends_far & (slot == far_from) & jnp.logical_not(spared & (f < DETOURS)))
        def _():
            forward_far(f).start()

        @pl.when((slot == FAR) & (f == 0))
        def _():
            pl.when(has_far)(lambda: wait_offsets(FAR))
            put_aug(FAR, tables(offs[FAR : FAR + 1]), 0)

    def deliver(slot, f):
        @pl.when(slot == FAR)
        def _():
            out_ref[f] = acc[f].T * scale

    def sent():
        off_partner.wait_send()

        @pl.when(has_up)
        def _():
            for copy in off_up:
                copy.wait_send()

        @pl.when(has_down)
        def _():
            for copy in off_down:
                copy.wait_send()

        pl.when(sends_far & jnp.logical_not(spared))(lambda: off_far.wait_send())
        pl.when(detours)(lambda: off_detour.wait_send())
        pl.when(relays)(lambda: off_relay.wait_send())
        for f in range(nfreq):
            to_partner(f).wait_send()
            pl.when(has_up)(lambda: to_plus(f).wait_send())
            pl.when(has_down)(lambda: to_minus(f).wait_send())

    def step(i, carry):
        (slot0, f0), (slot1, f1) = (((slots >> (3 * i)) & 7, (freqs >> (2 * i)) & 3) for slots, freqs in codes)
        arrive(slot0, f0)
        arrive(slot1, f1)

        @pl.when((i == 2) & detours)
        def _():
            for n in range(DETOURS):
                detour(n).start()

        @pl.when(i == len(EVEN) // 2 - 1)
        def _():
            sent()

        @pl.when((i == 4) & relays)
        def _():
            off_detour.wait_recv()
            off_relay.start()
            for n in range(DETOURS):
                detour(n).wait_recv()
                relay(n).start()

        g0 = grads(slot0, f0)
        g1 = grads(slot1, f1)
        acc[f0] += terms(slot0, f0, g0)
        acc[f1] += terms(slot1, f1, g1)
        deliver(slot0, f0)
        deliver(slot1, f1)
        return carry

    lax.fori_loop(0, len(EVEN) // 2, step, 0)

    for f in range(nfreq):
        pl.when(has_up)(lambda: forward(P_SAME, f).wait_send())
        pl.when(has_down)(lambda: forward(M_SAME, f).wait_send())
        if f < DETOURS:
            pl.when(sends_far & jnp.logical_not(spared))(lambda: forward_far(f).wait_send())
            pl.when(detours)(lambda: detour(f).wait_send())
            pl.when(relays)(lambda: relay(f).wait_send())
        else:
            pl.when(sends_far)(lambda: forward_far(f).wait_send())


def local(ndev, spectra, offsets, bins):
    nfreq, nch, width = spectra.shape
    lanes = 128
    assert width == lanes and nch % lanes == 0 and nfreq % 2 == 0 and 8 * nfreq <= lanes
    assert (nch * spacing_metres) % period_metres == 0 and nfreq == 4
    hbm = pl.BlockSpec(memory_space=pltpu.HBM)
    args = (bins, offsets.reshape(nch // lanes, lanes), spectra)
    return pl.pallas_call(
        functools.partial(kernel, nfreq, nch, ndev),
        out_shape=jax.ShapeDtypeStruct((nfreq, nch, width), F32),
        in_specs=[hbm, hbm, hbm],
        out_specs=pl.BlockSpec(memory_space=pltpu.VMEM),
        scratch_shapes=[
            pltpu.VMEM((7, nfreq, nch, width), BF16),
            pltpu.VMEM((7, nch, lanes), BF16),
            pltpu.VMEM((nfreq, 2 * lanes, nch), BF16),
            pltpu.VMEM((nfreq, 2 * lanes, nch), BF16),
            pltpu.VMEM((nfreq, width, nch), F32),
            pltpu.VMEM((7, nch // lanes, lanes), jnp.int32),
            pltpu.SMEM((nfreq,), jnp.int32),
            pltpu.SemaphoreType.DMA((2,)),
            pltpu.SemaphoreType.DMA((nfreq,)),
            pltpu.SemaphoreType.DMA((7, nfreq)),
            pltpu.SemaphoreType.DMA((7, nfreq)),
            pltpu.SemaphoreType.DMA((7,)),
            pltpu.SemaphoreType.DMA((7,)),
            pltpu.VMEM((DETOURS, nch, width), BF16),
            pltpu.VMEM((nch // lanes, lanes), jnp.int32),
            pltpu.SemaphoreType.DMA((DETOURS + 1,)),
        ],
        compiler_params=pltpu.CompilerParams(
            collective_id=0, has_side_effects=True, vmem_limit_bytes=24 << 20),
    )(*(pltpu.with_memory_space_constraint(v, pltpu.HBM) for v in args))


def solution(mesh):
    return jax.shard_map(
        functools.partial(local, mesh.shape["ch"]),
        mesh=mesh,
        in_specs=(P(None, "ch", None), P("ch"), P()),
        out_specs=P(None, "ch", None),
        check_vma=False,
    )
```

```python
import functools
import math

import jax
import jax.numpy as jnp
from jax import lax
from jax.experimental import pallas as pl
from jax.experimental.pallas import tpu as pltpu
from jax.sharding import PartitionSpec as P

spacing_metres = 8
period_metres = 4096
model_amp = 0.5

F32 = jnp.float32
BF16 = jnp.bfloat16
MESH = pl.DeviceIdType.MESH

OWN, PARTNER, M_SAME, P_SAME, M_OTHER, P_OTHER, FAR = range(7)
TO_PARTNER, TO_PLUS, TO_MINUS, FWD_M, FWD_P, FWD_FAR, DETOUR = range(7)

PLANE, ROW = 16, 4
DETOURS = 1
ALONE = 4

def even(one, one_other, two, two_other):
    near = sum(([(one, f), (two, f), (one_other, f), (two_other, f)] for f in range(4)), [])
    return near + [(FAR, f) for f in range(4)]


def lopsided(early, early_other, late, late_other):
    start = [
        (early, 0), (early, 1), (early_other, 0), (early_other, 1), (early, 2), (late, 0), (early_other, 2),
        (late_other, 0), (early, 3), (late, 1), (early_other, 3), (late_other, 1)]
    return start + [
        (late, 2), (FAR, 0), (late_other, 2), (FAR, 1), (late, 3), (FAR, 2), (late_other, 3), (FAR, 3)]


M_FIRST, P_FIRST = (M_SAME, M_OTHER, P_SAME, P_OTHER), (P_SAME, P_OTHER, M_SAME, M_OTHER)
ORDERS = (even(*M_FIRST), even(*P_FIRST), lopsided(*P_FIRST), lopsided(*M_FIRST))


def packed(values, bits):
    return sum(v << (bits * i) for i, v in enumerate(values))


def dot(a, b):
    return lax.dot_general(a, b, (((1,), (0,)), ((), ())), preferred_element_type=F32)


def cos_sin(m):
    quarter = period_metres // 4
    turn = (m + quarter // 2) // quarter
    theta = (m - turn * quarter).astype(F32) * (2.0 * math.pi / period_metres)
    x = theta * theta
    s = theta * (1.0 + x * (-1.0 / 6 + x * (1.0 / 120 + x * (-1.0 / 5040 + x * (1.0 / 362880)))))
    c = 1.0 + x * (-0.5 + x * (1.0 / 24 + x * (-1.0 / 720 + x * (1.0 / 40320))))
    turn = turn & 3
    odd = (turn & 1) == 1
    cos = jnp.where(odd, s, c)
    sin = jnp.where(odd, c, s)
    cos = jnp.where((turn == 1) | (turn == 2), -cos, cos)
    sin = jnp.where(turn >= 2, -sin, sin)
    return cos, sin


def split(v):
    high = v.astype(BF16).astype(F32)
    return high, v - high


def kernel(nfreq, nch, ndev, bins_hbm, off_ref, spec_ref, out_ref, blk, aug, wre, wim, acc, offs, bins_ref,
           in_sem, local_sem, send_sem, recv_sem, off_send, off_recv, via, via_off, via_recv, token):
    lanes = 128
    groups = nch // lanes
    me = lax.axis_index("ch")
    nchip = ndev // 2
    chip = me // 2
    core = me - 2 * chip
    up = jnp.minimum(chip + 1, nchip - 1)
    down = jnp.maximum(chip - 1, 0)
    has_up = chip < nchip - 1
    has_down = chip >= 1
    partner = 2 * chip + (1 - core)
    plus_same, plus_other = 2 * up + core, 2 * up + (1 - core)
    minus_same, minus_other = 2 * down + core, 2 * down + (1 - core)
    upward = core == 1
    far_to = jnp.where(upward, plus_other, minus_other)
    far_from = jnp.where(upward, M_SAME, P_SAME)
    sends_far = has_up & has_down
    has_far = jnp.where(upward, chip < nchip - 2, chip >= 2)
    def stepped(place):
        return lax.rem(place + PLANE, PLANE) == 0

    spared = sends_far & jnp.where(upward, stepped(chip + 1), stepped(chip))
    detours = jnp.where(upward, stepped(chip + 3) & (chip + 4 < nchip), stepped(chip - 2) & (chip >= 4))
    relays = jnp.where(upward, stepped(chip - 1) & (chip >= 4), stepped(chip + 2) & (chip + 4 < nchip))
    four_up, four_down = 2 * jnp.minimum(chip + 4, nchip - 1) + core, 2 * jnp.maximum(chip - 4, 0) + core
    detour_to = jnp.where(upward, four_up, four_down)
    detour_from = jnp.where(upward, P_SAME, M_SAME)
    relay_from = jnp.where(upward, four_down, four_up)
    relay_to = jnp.where(upward, minus_other, plus_other)
    crosses = jnp.where(upward, stepped(chip + 2) & (chip + 3 < nchip), stepped(chip - 1) & (chip >= 3))
    cross_to = jnp.where(
        upward, 2 * jnp.minimum(chip + 3, nchip - 1), 2 * jnp.maximum(chip - 3, 0) + 1)
    crossed = sends_far & jnp.where(upward, stepped(chip), stepped(chip + 1))
    tells = jnp.where(upward, stepped(chip + 1) & has_up, stepped(chip) & has_down)
    told = jnp.where(upward, minus_same, plus_same)
    late_m = (lax.rem(chip, PLANE) == 0) & has_down
    late_p = (lax.rem(chip + 1, PLANE) == 0) & has_up
    edge = late_m | late_p
    p_early = lax.rem(chip, ROW) < 2

    def coded(units, field, bits):
        m_first, p_first, m, p = (packed([unit[field] for unit in order[units]], bits) for order in ORDERS)
        return jnp.where(late_m, m, jnp.where(late_p, p, jnp.where(p_early, p_first, m_first)))

    units = len(ORDERS[0])
    codes = [(coded(slice(n, None, 2), 0, 3), coded(slice(n, None, 2), 1, 2)) for n in range(2)]
    alone = coded(slice(units - ALONE, None), 0, 3), coded(slice(units - ALONE, None), 1, 2)
    singles = jnp.where(edge, 0, ALONE)
    pairs = (units - singles) // 2

    def unit_at(code, i):
        return (code[0] >> (3 * i)) & 7, (code[1] >> (2 * i)) & 3

    barrier = pltpu.get_barrier_semaphore()

    def greet(peer):
        pl.semaphore_signal(barrier, inc=1, device_id=(peer,), device_id_type=MESH)

    @pl.when(has_up)
    def _():
        greet(plus_same)
        greet(plus_other)

    @pl.when(has_down)
    def _():
        greet(minus_same)
        greet(minus_other)

    greet(partner)
    pl.when(detours)(lambda: greet(detour_to))
    pl.when(relays)(lambda: greet(relay_from))

    def own_load(f):
        return pltpu.make_async_copy(spec_ref.at[f], blk.at[OWN, f], local_sem.at[f])

    bins_load = pltpu.make_async_copy(bins_hbm, bins_ref, in_sem.at[0])
    off_load = pltpu.make_async_copy(off_ref, offs.at[OWN], in_sem.at[1])
    bins_load.start()
    off_load.start()
    for f in range(nfreq):
        own_load(f).start()

    def clear(slots, freqs):
        for slot in slots:
            offs[slot] = jnp.zeros(offs.shape[1:], offs.dtype)
            for f in range(freqs):
                blk[slot, f] = jnp.zeros(blk.shape[2:], blk.dtype)

    @pl.when(jnp.logical_not(has_down))
    def _():
        clear((M_SAME, M_OTHER), nfreq)

    @pl.when(jnp.logical_not(has_up))
    def _():
        clear((P_SAME, P_OTHER), nfreq)

    @pl.when(jnp.logical_not(has_far))
    def _():
        clear((FAR,), nfreq)

    aug[...] = jnp.zeros_like(aug)
    wre[:, lanes:, :] = jnp.zeros((nfreq, wre.shape[1] - lanes, nch), BF16)
    wim[:, lanes:, :] = jnp.zeros((nfreq, wim.shape[1] - lanes, nch), BF16)

    def send(kind, f, src, slot, to):
        return pltpu.make_async_remote_copy(
            src_ref=src, dst_ref=blk.at[slot, f], send_sem=send_sem.at[kind, f],
            recv_sem=recv_sem.at[slot, f], device_id=(to,), device_id_type=MESH)

    def to_plus(f):
        return send(TO_PLUS, f, spec_ref.at[f], M_SAME, plus_same)

    def to_minus(f):
        return send(TO_MINUS, f, spec_ref.at[f], P_SAME, minus_same)

    def to_partner(f):
        return send(TO_PARTNER, f, spec_ref.at[f], PARTNER, partner)

    def forward(slot, f):
        return send(slot + FWD_M - M_SAME, f, blk.at[slot, f], slot + M_OTHER - M_SAME, partner)

    def forward_far(f):
        return send(FWD_FAR, f, blk.at[far_from, f], FAR, far_to)

    def detour(f):
        return pltpu.make_async_remote_copy(
            src_ref=blk.at[detour_from, f], dst_ref=via.at[f], send_sem=send_sem.at[DETOUR, f],
            recv_sem=via_recv.at[f], device_id=(detour_to,), device_id_type=MESH)

    def cross():
        return send(DETOUR, nfreq - 1, blk.at[detour_from, nfreq - 1], FAR, cross_to)

    def relay(f):
        return send(DETOUR, f, via.at[f], FAR, relay_to)

    def off_copy(n, src, slot, to):
        return pltpu.make_async_remote_copy(
            src_ref=src, dst_ref=offs.at[slot], send_sem=off_send.at[n],
            recv_sem=off_recv.at[slot], device_id=(to,), device_id_type=MESH)

    off_partner = off_copy(0, off_ref, PARTNER, partner)
    off_up = (off_copy(1, off_ref, M_SAME, plus_same), off_copy(3, off_ref, M_OTHER, plus_other))
    off_down = (off_copy(2, off_ref, P_SAME, minus_same), off_copy(4, off_ref, P_OTHER, minus_other))
    off_far = off_copy(5, offs.at[far_from], FAR, far_to)
    off_detour = pltpu.make_async_remote_copy(
        src_ref=offs.at[detour_from], dst_ref=via_off, send_sem=off_send.at[6],
        recv_sem=via_recv.at[DETOURS], device_id=(detour_to,), device_id_type=MESH)
    off_relay = off_copy(6, via_off, FAR, relay_to)

    def wait_block(slot, f):
        send(TO_PLUS, f, spec_ref.at[f], slot, partner).wait_recv()

    def wait_offsets(slot):
        off_copy(0, off_ref, slot, partner).wait_recv()

    row = lax.broadcasted_iota(jnp.int32, (8, lanes), 0)
    part = row & 3

    def pick(parts, a, b, c, d):
        return jnp.where(parts == 0, a, jnp.where(parts == 1, b, jnp.where(parts == 2, c, d)))

    def tables(off):
        shape = off.shape
        place = lax.broadcasted_iota(jnp.int32, shape, 1) * lanes + lax.broadcasted_iota(jnp.int32, shape, 2)
        pos = place * spacing_metres + off
        result = []
        for f in range(nfreq):
            cos, sin = cos_sin((bins_ref[f] * pos) & (period_metres - 1))
            result.append(split(cos) + split(sin))
        return result

    def put_aug(slot, table, n):
        for g in range(groups):
            rows = []
            for f in range(nfreq):
                ch, cl, sh, sl = (v[n, g : g + 1, :] for v in table[f])
                rows.append(pick(part, ch, cl, sh, sl))
            block = jnp.concatenate(rows, axis=0)
            aug[slot, g * lanes : (g + 1) * lanes, 0 : 8 * nfreq] = block.T.astype(BF16)

    bins_load.wait()
    off_load.wait()
    own_table = tables(offs[OWN : OWN + 1])
    put_aug(OWN, own_table, 0)
    late = row >= 4
    cosine = part < 2
    nothing = jnp.zeros((8, lanes), F32)
    for g in range(groups):
        for f in range(nfreq):
            ch, cl, sh, sl = (v[0, g : g + 1, :] for v in own_table[f])
            cos = jnp.where(late, cl, ch)
            sin = jnp.where(late, sl, sh)
            real = jnp.where(cosine, cos, sin) * (-model_amp)
            imag = jnp.where(cosine, sin, -cos) * model_amp
            cols = slice(g * lanes, (g + 1) * lanes)
            rows = slice(lanes, lanes + 8 * nfreq)
            wre[f, rows, cols] = jnp.concatenate(
                [real if n == f else nothing for n in range(nfreq)], axis=0).astype(BF16)
            wim[f, rows, cols] = jnp.concatenate(
                [imag if n == f else nothing for n in range(nfreq)], axis=0).astype(BF16)

    def open_links():
        greeted = 1 + 2 * has_up.astype(jnp.int32) + 2 * has_down.astype(jnp.int32)
        greeted += (detours | relays).astype(jnp.int32)
        pl.semaphore_wait(barrier, greeted)

        @pl.when(has_up)
        def _():
            to_plus(0).start()
            for copy in off_up:
                copy.start()

        @pl.when(has_down)
        def _():
            to_minus(0).start()
            for copy in off_down:
                copy.start()

        off_partner.start()
        to_partner(0).start()
        for f in range(1, nfreq):
            pl.when(has_up)(lambda f=f: to_plus(f).start())
            pl.when(has_down)(lambda f=f: to_minus(f).start())
            to_partner(f).start()

    pl.when(jnp.logical_not(edge))(open_links)

    half = lanes // 2
    scale = 1.0 / half

    def transposed(slot, f):
        t = blk[slot, f].T
        return t, jnp.concatenate([-t[half:], t[:half]], axis=0)

    def grads(slot, f):
        x = jnp.concatenate([blk[slot, f], aug[slot]], axis=1)
        real = jnp.tanh(dot(x, wre[f])).astype(BF16)
        imag = jnp.tanh(dot(x, wim[f])).astype(BF16)
        return real, imag

    def terms(slot, f, g):
        t, swapped = transposed(slot, f)
        return dot(t, g[0]) + dot(swapped, g[1])

    def own_step(i, carry):
        fs = [2 * i, 2 * i + 1]
        for f in fs:
            own_load(f).wait()
            t, swapped = transposed(OWN, f)
            wre[f, :lanes, :] = t * jnp.array(scale, BF16)
            wim[f, :lanes, :] = swapped * jnp.array(-scale, BF16)
        g = [grads(OWN, f) for f in fs]
        for f, v in zip(fs, g):
            acc[f] = 2.0 * terms(OWN, f, v)
        return carry

    lax.fori_loop(0, nfreq // 2, own_step, 0)
    pl.when(edge)(open_links)

    wait_offsets(PARTNER)
    put_aug(PARTNER, tables(offs[PARTNER : PARTNER + 1]), 0)

    def partner_step(i, carry):
        fs = [2 * i, 2 * i + 1]
        for f in fs:
            wait_block(PARTNER, f)
        g = [grads(PARTNER, f) for f in fs]
        for f, v in zip(fs, g):
            acc[f] += terms(PARTNER, f, v)
        return carry

    lax.fori_loop(0, nfreq // 2, partner_step, 0)

    @pl.when(has_down)
    def _():
        wait_offsets(M_SAME)
        wait_offsets(M_OTHER)

    @pl.when(has_up)
    def _():
        wait_offsets(P_SAME)
        wait_offsets(P_OTHER)

    @pl.when(sends_far & jnp.logical_not(spared))
    def _():
        off_far.start()

    pl.when(detours)(lambda: off_detour.start())

    table = tables(offs[M_SAME : P_OTHER + 1])
    for slot in range(M_SAME, P_OTHER + 1):
        put_aug(slot, table, slot - M_SAME)

    def arrive(slot, f):
        there = jnp.where(slot == FAR, has_far, jnp.where((slot & 1) == 1, has_up, has_down))

        @pl.when(there)
        def _():
            wait_block(slot, f)

        @pl.when(there & (slot <= P_SAME))
        def _():
            forward(slot, f).start()

        @pl.when(tells & (slot == detour_from) & (f == 0))
        def _():
            pl.semaphore_signal(token, inc=1, device_id=(told,), device_id_type=MESH)

        elsewhere = (spared & (f < DETOURS)) | (crossed & (f == nfreq - 1))

        @pl.when(sends_far & (slot == far_from) & jnp.logical_not(elsewhere))
        def _():
            forward_far(f).start()

        @pl.when((slot == FAR) & (f == 0))
        def _():
            pl.when(has_far)(lambda: wait_offsets(FAR))
            put_aug(FAR, tables(offs[FAR : FAR + 1]), 0)

    def deliver(slot, f):
        @pl.when(slot == FAR)
        def _():
            out_ref[f] = acc[f].T * scale

    def sent():
        off_partner.wait_send()

        @pl.when(has_up)
        def _():
            for copy in off_up:
                copy.wait_send()

        @pl.when(has_down)
        def _():
            for copy in off_down:
                copy.wait_send()

        pl.when(sends_far & jnp.logical_not(spared))(lambda: off_far.wait_send())
        pl.when(detours)(lambda: off_detour.wait_send())
        pl.when(relays)(lambda: off_relay.wait_send())
        for f in range(nfreq):
            to_partner(f).wait_send()
            pl.when(has_up)(lambda: to_plus(f).wait_send())
            pl.when(has_down)(lambda: to_minus(f).wait_send())

    def step(i, carry):
        (slot0, f0), (slot1, f1) = (unit_at(code, i) for code in codes)
        arrive(slot0, f0)
        arrive(slot1, f1)

        for n in range(DETOURS):
            pl.when((i == 2 * n) & detours)(lambda n=n: detour(n).start())

        @pl.when((i == 2) & relays)
        def _():
            off_detour.wait_recv()
            off_relay.start()

        for n in range(DETOURS):
            @pl.when((i == 2 * n + 2) & relays)
            def _():
                detour(n).wait_recv()
                relay(n).start()

        @pl.when((i == 2 * nfreq - 2) & crosses)
        def _():
            pl.semaphore_wait(token, 1)
            cross().start()

        g0 = grads(slot0, f0)
        g1 = grads(slot1, f1)
        acc[f0] += terms(slot0, f0, g0)
        acc[f1] += terms(slot1, f1, g1)
        deliver(slot0, f0)
        deliver(slot1, f1)
        return carry

    lax.fori_loop(0, pairs, step, 0)
    sent()

    def last_step(i, carry):
        slot, f = unit_at(alone, i)
        arrive(slot, f)
        acc[f] += terms(slot, f, grads(slot, f))
        deliver(slot, f)
        return carry

    lax.fori_loop(0, singles, last_step, 0)

    for f in range(nfreq):
        pl.when(has_up)(lambda: forward(P_SAME, f).wait_send())
        pl.when(has_down)(lambda: forward(M_SAME, f).wait_send())
        if f < DETOURS:
            pl.when(sends_far & jnp.logical_not(spared))(lambda: forward_far(f).wait_send())
            pl.when(detours)(lambda: detour(f).wait_send())
            pl.when(relays)(lambda: relay(f).wait_send())
        elif f < nfreq - 1:
            pl.when(sends_far)(lambda: forward_far(f).wait_send())
        else:
            pl.when(sends_far & jnp.logical_not(crossed))(lambda: forward_far(f).wait_send())
            pl.when(crosses)(lambda: cross().wait_send())


def local(ndev, spectra, offsets, bins):
    nfreq, nch, width = spectra.shape
    lanes = 128
    assert width == lanes and nch % lanes == 0 and nfreq % 2 == 0 and 8 * nfreq <= lanes
    assert (nch * spacing_metres) % period_metres == 0 and nfreq == 4
    hbm = pl.BlockSpec(memory_space=pltpu.HBM)
    args = (bins, offsets.reshape(nch // lanes, lanes), spectra)
    return pl.pallas_call(
        functools.partial(kernel, nfreq, nch, ndev),
        out_shape=jax.ShapeDtypeStruct((nfreq, nch, width), F32),
        in_specs=[hbm, hbm, hbm],
        out_specs=pl.BlockSpec(memory_space=pltpu.VMEM),
        scratch_shapes=[
            pltpu.VMEM((7, nfreq, nch, width), BF16),
            pltpu.VMEM((7, nch, lanes), BF16),
            pltpu.VMEM((nfreq, 2 * lanes, nch), BF16),
            pltpu.VMEM((nfreq, 2 * lanes, nch), BF16),
            pltpu.VMEM((nfreq, width, nch), F32),
            pltpu.VMEM((7, nch // lanes, lanes), jnp.int32),
            pltpu.SMEM((nfreq,), jnp.int32),
            pltpu.SemaphoreType.DMA((2,)),
            pltpu.SemaphoreType.DMA((nfreq,)),
            pltpu.SemaphoreType.DMA((7, nfreq)),
            pltpu.SemaphoreType.DMA((7, nfreq)),
            pltpu.SemaphoreType.DMA((7,)),
            pltpu.SemaphoreType.DMA((7,)),
            pltpu.VMEM((DETOURS, nch, width), BF16),
            pltpu.VMEM((nch // lanes, lanes), jnp.int32),
            pltpu.SemaphoreType.DMA((DETOURS + 1,)),
            pltpu.SemaphoreType.REGULAR,
        ],
        compiler_params=pltpu.CompilerParams(
            collective_id=0, has_side_effects=True, vmem_limit_bytes=24 << 20),
    )(*(pltpu.with_memory_space_constraint(v, pltpu.HBM) for v in args))


def solution(mesh):
    return jax.shard_map(
        functools.partial(local, mesh.shape["ch"]),
        mesh=mesh,
        in_specs=(P(None, "ch", None), P("ch"), P()),
        out_specs=P(None, "ch", None),
        check_vma=False,
    )
```

```python
import functools
import math

import jax
import jax.numpy as jnp
from jax import lax
from jax.experimental import pallas as pl
from jax.experimental.pallas import tpu as pltpu
from jax.sharding import PartitionSpec as P

spacing_metres = 8
period_metres = 4096
model_amp = 0.5

F32 = jnp.float32
BF16 = jnp.bfloat16
MESH = pl.DeviceIdType.MESH

OWN, PARTNER, M_SAME, P_SAME, M_OTHER, P_OTHER, FAR = range(7)
TO_PARTNER, TO_PLUS, TO_MINUS, FWD_M, FWD_P, FWD_FAR, DETOUR = range(7)

PLANE, ROW = 16, 4
DETOURS, DETOURS_DOWN = 2, 1
ALONE = 4

def even(one, one_other, two, two_other):
    near = sum(([(one, f), (two, f), (one_other, f), (two_other, f)] for f in range(4)), [])
    return near + [(FAR, f) for f in range(4)]


def lopsided(early, early_other, late, late_other):
    start = [
        (early, 0), (early, 1), (early_other, 0), (early_other, 1), (early, 2), (late, 0), (early_other, 2),
        (late_other, 0), (early, 3), (late, 1), (early_other, 3), (late_other, 1)]
    return start + [
        (late, 2), (FAR, 0), (late_other, 2), (late, 3), (late_other, 3), (FAR, 1), (FAR, 2), (FAR, 3)]


M_FIRST, P_FIRST = (M_SAME, M_OTHER, P_SAME, P_OTHER), (P_SAME, P_OTHER, M_SAME, M_OTHER)
ORDERS = (even(*M_FIRST), even(*P_FIRST), lopsided(*P_FIRST), lopsided(*M_FIRST))


def packed(values, bits):
    return sum(v << (bits * i) for i, v in enumerate(values))


def dot(a, b):
    return lax.dot_general(a, b, (((1,), (0,)), ((), ())), preferred_element_type=F32)


def cos_sin(m):
    quarter = period_metres // 4
    turn = (m + quarter // 2) // quarter
    theta = (m - turn * quarter).astype(F32) * (2.0 * math.pi / period_metres)
    x = theta * theta
    s = theta * (1.0 + x * (-1.0 / 6 + x * (1.0 / 120 + x * (-1.0 / 5040 + x * (1.0 / 362880)))))
    c = 1.0 + x * (-0.5 + x * (1.0 / 24 + x * (-1.0 / 720 + x * (1.0 / 40320))))
    turn = turn & 3
    odd = (turn & 1) == 1
    cos = jnp.where(odd, s, c)
    sin = jnp.where(odd, c, s)
    cos = jnp.where((turn == 1) | (turn == 2), -cos, cos)
    sin = jnp.where(turn >= 2, -sin, sin)
    return cos, sin


def split(v):
    high = v.astype(BF16).astype(F32)
    return high, v - high


def kernel(nfreq, nch, ndev, bins_hbm, off_ref, spec_ref, out_ref, blk, aug, wre, wim, acc, offs, bins_ref,
           in_sem, local_sem, send_sem, recv_sem, off_send, off_recv, via, via_off, via_recv, token):
    lanes = 128
    groups = nch // lanes
    me = lax.axis_index("ch")
    nchip = ndev // 2
    chip = me // 2
    core = me - 2 * chip
    up = jnp.minimum(chip + 1, nchip - 1)
    down = jnp.maximum(chip - 1, 0)
    has_up = chip < nchip - 1
    has_down = chip >= 1
    partner = 2 * chip + (1 - core)
    plus_same, plus_other = 2 * up + core, 2 * up + (1 - core)
    minus_same, minus_other = 2 * down + core, 2 * down + (1 - core)
    upward = core == 1
    far_to = jnp.where(upward, plus_other, minus_other)
    far_from = jnp.where(upward, M_SAME, P_SAME)
    sends_far = has_up & has_down
    has_far = jnp.where(upward, chip < nchip - 2, chip >= 2)
    def stepped(place):
        return lax.rem(place + PLANE, PLANE) == 0

    spared_bins = jnp.where(upward, DETOURS, DETOURS_DOWN)
    spared = sends_far & jnp.where(upward, stepped(chip + 1), stepped(chip))
    detours = jnp.where(upward, stepped(chip + 3) & (chip + 4 < nchip), stepped(chip - 2) & (chip >= 4))
    relays = jnp.where(upward, stepped(chip - 1) & (chip >= 4), stepped(chip + 2) & (chip + 4 < nchip))
    four_up, four_down = 2 * jnp.minimum(chip + 4, nchip - 1) + core, 2 * jnp.maximum(chip - 4, 0) + core
    detour_to = jnp.where(upward, four_up, four_down)
    detour_from = jnp.where(upward, P_SAME, M_SAME)
    relay_from = jnp.where(upward, four_down, four_up)
    relay_to = jnp.where(upward, minus_other, plus_other)
    crosses = jnp.where(upward, stepped(chip + 2) & (chip + 3 < nchip), stepped(chip - 1) & (chip >= 3))
    cross_to = jnp.where(
        upward, 2 * jnp.minimum(chip + 3, nchip - 1), 2 * jnp.maximum(chip - 3, 0) + 1)
    crossed = sends_far & jnp.where(upward, stepped(chip), stepped(chip + 1))
    tells = jnp.where(upward, stepped(chip + 1) & has_up, stepped(chip) & has_down)
    told = jnp.where(upward, minus_same, plus_same)
    late_m = (lax.rem(chip, PLANE) == 0) & has_down
    late_p = (lax.rem(chip + 1, PLANE) == 0) & has_up
    edge = late_m | late_p
    p_early = lax.rem(chip, ROW) < 2

    def coded(units, field, bits):
        m_first, p_first, m, p = (packed([unit[field] for unit in order[units]], bits) for order in ORDERS)
        return jnp.where(late_m, m, jnp.where(late_p, p, jnp.where(p_early, p_first, m_first)))

    units = len(ORDERS[0])
    codes = [(coded(slice(n, None, 2), 0, 3), coded(slice(n, None, 2), 1, 2)) for n in range(2)]
    alone = coded(slice(units - ALONE, None), 0, 3), coded(slice(units - ALONE, None), 1, 2)
    singles = jnp.where(edge, 0, ALONE)
    pairs = (units - singles) // 2

    def unit_at(code, i):
        return (code[0] >> (3 * i)) & 7, (code[1] >> (2 * i)) & 3

    barrier = pltpu.get_barrier_semaphore()

    def greet(peer):
        pl.semaphore_signal(barrier, inc=1, device_id=(peer,), device_id_type=MESH)

    @pl.when(has_up)
    def _():
        greet(plus_same)
        greet(plus_other)

    @pl.when(has_down)
    def _():
        greet(minus_same)
        greet(minus_other)

    greet(partner)
    pl.when(detours)(lambda: greet(detour_to))
    pl.when(relays)(lambda: greet(relay_from))

    def own_load(f):
        return pltpu.make_async_copy(spec_ref.at[f], blk.at[OWN, f], local_sem.at[f])

    bins_load = pltpu.make_async_copy(bins_hbm, bins_ref, in_sem.at[0])
    off_load = pltpu.make_async_copy(off_ref, offs.at[OWN], in_sem.at[1])
    bins_load.start()
    off_load.start()
    for f in range(nfreq):
        own_load(f).start()

    def clear(slots, freqs):
        for slot in slots:
            offs[slot] = jnp.zeros(offs.shape[1:], offs.dtype)
            for f in range(freqs):
                blk[slot, f] = jnp.zeros(blk.shape[2:], blk.dtype)

    @pl.when(jnp.logical_not(has_down))
    def _():
        clear((M_SAME, M_OTHER), nfreq)

    @pl.when(jnp.logical_not(has_up))
    def _():
        clear((P_SAME, P_OTHER), nfreq)

    @pl.when(jnp.logical_not(has_far))
    def _():
        clear((FAR,), nfreq)

    aug[...] = jnp.zeros_like(aug)
    wre[:, lanes:, :] = jnp.zeros((nfreq, wre.shape[1] - lanes, nch), BF16)
    wim[:, lanes:, :] = jnp.zeros((nfreq, wim.shape[1] - lanes, nch), BF16)

    def send(kind, f, src, slot, to):
        return pltpu.make_async_remote_copy(
            src_ref=src, dst_ref=blk.at[slot, f], send_sem=send_sem.at[kind, f],
            recv_sem=recv_sem.at[slot, f], device_id=(to,), device_id_type=MESH)

    def to_plus(f):
        return send(TO_PLUS, f, blk.at[OWN, f], M_SAME, plus_same)

    def to_minus(f):
        return send(TO_MINUS, f, blk.at[OWN, f], P_SAME, minus_same)

    def to_partner(f):
        return send(TO_PARTNER, f, blk.at[OWN, f], PARTNER, partner)

    def forward(slot, f):
        return send(slot + FWD_M - M_SAME, f, blk.at[slot, f], slot + M_OTHER - M_SAME, partner)

    def forward_far(f):
        return send(FWD_FAR, f, blk.at[far_from, f], FAR, far_to)

    def detour(f):
        return pltpu.make_async_remote_copy(
            src_ref=blk.at[detour_from, f], dst_ref=via.at[f], send_sem=send_sem.at[DETOUR, f],
            recv_sem=via_recv.at[f], device_id=(detour_to,), device_id_type=MESH)

    def cross():
        return send(DETOUR, nfreq - 1, blk.at[detour_from, nfreq - 1], FAR, cross_to)

    def relay(f):
        return send(DETOUR, f, via.at[f], FAR, relay_to)

    def off_copy(n, src, slot, to):
        return pltpu.make_async_remote_copy(
            src_ref=src, dst_ref=offs.at[slot], send_sem=off_send.at[n],
            recv_sem=off_recv.at[slot], device_id=(to,), device_id_type=MESH)

    off_partner = off_copy(0, off_ref, PARTNER, partner)
    off_up = (off_copy(1, off_ref, M_SAME, plus_same), off_copy(3, off_ref, M_OTHER, plus_other))
    off_down = (off_copy(2, off_ref, P_SAME, minus_same), off_copy(4, off_ref, P_OTHER, minus_other))
    off_far = off_copy(5, offs.at[far_from], FAR, far_to)
    off_detour = pltpu.make_async_remote_copy(
        src_ref=offs.at[detour_from], dst_ref=via_off, send_sem=off_send.at[6],
        recv_sem=via_recv.at[DETOURS], device_id=(detour_to,), device_id_type=MESH)
    off_relay = off_copy(6, via_off, FAR, relay_to)

    def wait_block(slot, f):
        send(TO_PLUS, f, spec_ref.at[f], slot, partner).wait_recv()

    def wait_offsets(slot):
        off_copy(0, off_ref, slot, partner).wait_recv()

    row = lax.broadcasted_iota(jnp.int32, (8, lanes), 0)
    part = row & 3

    def pick(parts, a, b, c, d):
        return jnp.where(parts == 0, a, jnp.where(parts == 1, b, jnp.where(parts == 2, c, d)))

    def tables(off):
        shape = off.shape
        place = lax.broadcasted_iota(jnp.int32, shape, 1) * lanes + lax.broadcasted_iota(jnp.int32, shape, 2)
        pos = place * spacing_metres + off
        result = []
        for f in range(nfreq):
            cos, sin = cos_sin((bins_ref[f] * pos) & (period_metres - 1))
            result.append(split(cos) + split(sin))
        return result

    def put_aug(slot, table, n):
        for g in range(groups):
            rows = []
            for f in range(nfreq):
                ch, cl, sh, sl = (v[n, g : g + 1, :] for v in table[f])
                rows.append(pick(part, ch, cl, sh, sl))
            block = jnp.concatenate(rows, axis=0)
            aug[slot, g * lanes : (g + 1) * lanes, 0 : 8 * nfreq] = block.T.astype(BF16)

    bins_load.wait()
    off_load.wait()
    own_table = tables(offs[OWN : OWN + 1])
    put_aug(OWN, own_table, 0)
    late = row >= 4
    cosine = part < 2
    nothing = jnp.zeros((8, lanes), F32)
    for g in range(groups):
        for f in range(nfreq):
            ch, cl, sh, sl = (v[0, g : g + 1, :] for v in own_table[f])
            cos = jnp.where(late, cl, ch)
            sin = jnp.where(late, sl, sh)
            real = jnp.where(cosine, cos, sin) * (-model_amp)
            imag = jnp.where(cosine, sin, -cos) * model_amp
            cols = slice(g * lanes, (g + 1) * lanes)
            rows = slice(lanes, lanes + 8 * nfreq)
            wre[f, rows, cols] = jnp.concatenate(
                [real if n == f else nothing for n in range(nfreq)], axis=0).astype(BF16)
            wim[f, rows, cols] = jnp.concatenate(
                [imag if n == f else nothing for n in range(nfreq)], axis=0).astype(BF16)

    def open_links():
        greeted = 1 + 2 * has_up.astype(jnp.int32) + 2 * has_down.astype(jnp.int32)
        greeted += (detours | relays).astype(jnp.int32)
        pl.semaphore_wait(barrier, greeted)

        @pl.when(has_up)
        def _():
            to_plus(0).start()
            for copy in off_up:
                copy.start()

        @pl.when(has_down)
        def _():
            to_minus(0).start()
            for copy in off_down:
                copy.start()

        off_partner.start()
        to_partner(0).start()
        for f in range(1, nfreq):
            pl.when(has_up)(lambda f=f: to_plus(f).start())
            pl.when(has_down)(lambda f=f: to_minus(f).start())
            to_partner(f).start()

    for f in range(nfreq):
        own_load(f).wait()
    pl.when(jnp.logical_not(edge))(open_links)

    half = lanes // 2
    scale = 1.0 / half

    def transposed(slot, f):
        t = blk[slot, f].T
        return t, jnp.concatenate([-t[half:], t[:half]], axis=0)

    def grads(slot, f):
        x = jnp.concatenate([blk[slot, f], aug[slot]], axis=1)
        real = jnp.tanh(dot(x, wre[f])).astype(BF16)
        imag = jnp.tanh(dot(x, wim[f])).astype(BF16)
        return real, imag

    def terms(slot, f, g):
        t, swapped = transposed(slot, f)
        return dot(t, g[0]) + dot(swapped, g[1])

    def own_step(i, carry):
        fs = [2 * i, 2 * i + 1]
        for f in fs:
            t, swapped = transposed(OWN, f)
            wre[f, :lanes, :] = t * jnp.array(scale, BF16)
            wim[f, :lanes, :] = swapped * jnp.array(-scale, BF16)
        g = [grads(OWN, f) for f in fs]
        for f, v in zip(fs, g):
            acc[f] = 2.0 * terms(OWN, f, v)
        return carry

    lax.fori_loop(0, nfreq // 2, own_step, 0)
    pl.when(edge)(open_links)

    wait_offsets(PARTNER)
    put_aug(PARTNER, tables(offs[PARTNER : PARTNER + 1]), 0)

    def partner_step(i, carry):
        fs = [2 * i, 2 * i + 1]
        for f in fs:
            wait_block(PARTNER, f)
        g = [grads(PARTNER, f) for f in fs]
        for f, v in zip(fs, g):
            acc[f] += terms(PARTNER, f, v)
        return carry

    lax.fori_loop(0, nfreq // 2, partner_step, 0)

    @pl.when(has_down)
    def _():
        wait_offsets(M_SAME)
        wait_offsets(M_OTHER)

    @pl.when(has_up)
    def _():
        wait_offsets(P_SAME)
        wait_offsets(P_OTHER)

    @pl.when(sends_far & jnp.logical_not(spared))
    def _():
        off_far.start()

    pl.when(detours)(lambda: off_detour.start())

    table = tables(offs[M_SAME : P_OTHER + 1])
    for slot in range(M_SAME, P_OTHER + 1):
        put_aug(slot, table, slot - M_SAME)

    def arrive(slot, f):
        there = jnp.where(slot == FAR, has_far, jnp.where((slot & 1) == 1, has_up, has_down))

        @pl.when(there)
        def _():
            wait_block(slot, f)

        @pl.when(there & (slot <= P_SAME))
        def _():
            forward(slot, f).start()

        @pl.when(tells & (slot == detour_from) & (f == 0))
        def _():
            pl.semaphore_signal(token, inc=1, device_id=(told,), device_id_type=MESH)

        elsewhere = (spared & (f < spared_bins)) | (crossed & (f == nfreq - 1))

        @pl.when(sends_far & (slot == far_from) & jnp.logical_not(elsewhere))
        def _():
            forward_far(f).start()

        @pl.when((slot == FAR) & (f == 0))
        def _():
            pl.when(has_far)(lambda: wait_offsets(FAR))
            put_aug(FAR, tables(offs[FAR : FAR + 1]), 0)

    def deliver(slot, f):
        @pl.when(slot == FAR)
        def _():
            out_ref[f] = acc[f].T * scale

    def sent():
        off_partner.wait_send()

        @pl.when(has_up)
        def _():
            for copy in off_up:
                copy.wait_send()

        @pl.when(has_down)
        def _():
            for copy in off_down:
                copy.wait_send()

        pl.when(sends_far & jnp.logical_not(spared))(lambda: off_far.wait_send())
        pl.when(detours)(lambda: off_detour.wait_send())
        pl.when(relays)(lambda: off_relay.wait_send())
        for f in range(nfreq):
            to_partner(f).wait_send()
            pl.when(has_up)(lambda: to_plus(f).wait_send())
            pl.when(has_down)(lambda: to_minus(f).wait_send())

    def step(i, carry):
        (slot0, f0), (slot1, f1) = (unit_at(code, i) for code in codes)
        arrive(slot0, f0)
        arrive(slot1, f1)

        for n in range(DETOURS):
            pl.when((i == 2 * n) & detours & (n < spared_bins))(lambda n=n: detour(n).start())

        @pl.when((i == 2) & relays)
        def _():
            off_detour.wait_recv()
            off_relay.start()

        for n in range(DETOURS):
            @pl.when((i == 2 * n + 2) & relays & (n < spared_bins))
            def _():
                detour(n).wait_recv()
                relay(n).start()

        @pl.when((i == 2 * nfreq - 2) & crosses)
        def _():
            pl.semaphore_wait(token, 1)
            cross().start()

        g0 = grads(slot0, f0)
        g1 = grads(slot1, f1)
        acc[f0] += terms(slot0, f0, g0)
        acc[f1] += terms(slot1, f1, g1)
        deliver(slot0, f0)
        deliver(slot1, f1)
        return carry

    lax.fori_loop(0, pairs, step, 0)
    sent()

    def last_step(i, carry):
        slot, f = unit_at(alone, i)
        arrive(slot, f)
        acc[f] += terms(slot, f, grads(slot, f))
        deliver(slot, f)
        return carry

    lax.fori_loop(0, singles, last_step, 0)

    for f in range(nfreq):
        pl.when(has_up)(lambda: forward(P_SAME, f).wait_send())
        pl.when(has_down)(lambda: forward(M_SAME, f).wait_send())
        if f < DETOURS:
            pl.when(sends_far & jnp.logical_not(spared & (f < spared_bins)))(lambda: forward_far(f).wait_send())
            pl.when(detours & (f < spared_bins))(lambda: detour(f).wait_send())
            pl.when(relays & (f < spared_bins))(lambda: relay(f).wait_send())
        elif f < nfreq - 1:
            pl.when(sends_far)(lambda: forward_far(f).wait_send())
        else:
            pl.when(sends_far & jnp.logical_not(crossed))(lambda: forward_far(f).wait_send())
            pl.when(crosses)(lambda: cross().wait_send())


def local(ndev, spectra, offsets, bins):
    nfreq, nch, width = spectra.shape
    lanes = 128
    assert width == lanes and nch % lanes == 0 and nfreq % 2 == 0 and 8 * nfreq <= lanes
    assert (nch * spacing_metres) % period_metres == 0 and nfreq == 4
    hbm = pl.BlockSpec(memory_space=pltpu.HBM)
    args = (bins, offsets.reshape(nch // lanes, lanes), spectra)
    return pl.pallas_call(
        functools.partial(kernel, nfreq, nch, ndev),
        out_shape=jax.ShapeDtypeStruct((nfreq, nch, width), F32),
        in_specs=[hbm, hbm, hbm],
        out_specs=pl.BlockSpec(memory_space=pltpu.VMEM),
        scratch_shapes=[
            pltpu.VMEM((7, nfreq, nch, width), BF16),
            pltpu.VMEM((7, nch, lanes), BF16),
            pltpu.VMEM((nfreq, 2 * lanes, nch), BF16),
            pltpu.VMEM((nfreq, 2 * lanes, nch), BF16),
            pltpu.VMEM((nfreq, width, nch), F32),
            pltpu.VMEM((7, nch // lanes, lanes), jnp.int32),
            pltpu.SMEM((nfreq,), jnp.int32),
            pltpu.SemaphoreType.DMA((2,)),
            pltpu.SemaphoreType.DMA((nfreq,)),
            pltpu.SemaphoreType.DMA((7, nfreq)),
            pltpu.SemaphoreType.DMA((7, nfreq)),
            pltpu.SemaphoreType.DMA((7,)),
            pltpu.SemaphoreType.DMA((7,)),
            pltpu.VMEM((DETOURS, nch, width), BF16),
            pltpu.VMEM((nch // lanes, lanes), jnp.int32),
            pltpu.SemaphoreType.DMA((DETOURS + 1,)),
            pltpu.SemaphoreType.REGULAR,
        ],
        compiler_params=pltpu.CompilerParams(
            collective_id=0, has_side_effects=True, vmem_limit_bytes=24 << 20),
    )(*(pltpu.with_memory_space_constraint(v, pltpu.HBM) for v in args))


def solution(mesh):
    return jax.shard_map(
        functools.partial(local, mesh.shape["ch"]),
        mesh=mesh,
        in_specs=(P(None, "ch", None), P("ch"), P()),
        out_specs=P(None, "ch", None),
        check_vma=False,
    )
```

```python
import functools
import math

import jax
import jax.numpy as jnp
from jax import lax
from jax.experimental import pallas as pl
from jax.experimental.pallas import tpu as pltpu
from jax.sharding import PartitionSpec as P

spacing_metres = 8
period_metres = 4096
model_amp = 0.5

F32 = jnp.float32
BF16 = jnp.bfloat16
MESH = pl.DeviceIdType.MESH

OWN, PARTNER, M_SAME, P_SAME, M_OTHER, P_OTHER, FAR = range(7)
TO_PARTNER, TO_PLUS, TO_MINUS, FWD_M, FWD_P, FWD_FAR, DETOUR = range(7)

PLANE, ROW = 16, 4
DETOURS, DETOURS_DOWN = 1, 1
ALONE = 4

def even(one, one_other, two, two_other):
    near = sum(([(one, f), (two, f), (one_other, f), (two_other, f)] for f in range(4)), [])
    return near + [(FAR, f) for f in range(4)]


def lopsided(early, early_other, late, late_other):
    start = [
        (early, 0), (early, 1), (early_other, 0), (early_other, 1), (early, 2), (late, 0), (early_other, 2),
        (late_other, 0), (early, 3), (late, 1), (early_other, 3), (late_other, 1)]
    return start + [
        (late, 2), (FAR, 0), (late_other, 2), (late, 3), (late_other, 3), (FAR, 1), (FAR, 2), (FAR, 3)]


M_FIRST, P_FIRST = (M_SAME, M_OTHER, P_SAME, P_OTHER), (P_SAME, P_OTHER, M_SAME, M_OTHER)
ORDERS = (even(*M_FIRST), even(*P_FIRST), lopsided(*P_FIRST), lopsided(*M_FIRST))


def packed(values, bits):
    return sum(v << (bits * i) for i, v in enumerate(values))


def dot(a, b):
    return lax.dot_general(a, b, (((1,), (0,)), ((), ())), preferred_element_type=F32)


def cos_sin(m):
    quarter = period_metres // 4
    turn = (m + quarter // 2) // quarter
    theta = (m - turn * quarter).astype(F32) * (2.0 * math.pi / period_metres)
    x = theta * theta
    s = theta * (1.0 + x * (-1.0 / 6 + x * (1.0 / 120 + x * (-1.0 / 5040 + x * (1.0 / 362880)))))
    c = 1.0 + x * (-0.5 + x * (1.0 / 24 + x * (-1.0 / 720 + x * (1.0 / 40320))))
    turn = turn & 3
    odd = (turn & 1) == 1
    cos = jnp.where(odd, s, c)
    sin = jnp.where(odd, c, s)
    cos = jnp.where((turn == 1) | (turn == 2), -cos, cos)
    sin = jnp.where(turn >= 2, -sin, sin)
    return cos, sin


def split(v):
    high = v.astype(BF16).astype(F32)
    return high, v - high


def kernel(nfreq, nch, ndev, bins_hbm, off_ref, spec_ref, out_ref, blk, aug, wre, wim, acc, offs, bins_ref,
           in_sem, local_sem, send_sem, recv_sem, off_send, off_recv, via, via_off, via_recv, token):
    lanes = 128
    groups = nch // lanes
    me = lax.axis_index("ch")
    nchip = ndev // 2
    chip = me // 2
    core = me - 2 * chip
    up = jnp.minimum(chip + 1, nchip - 1)
    down = jnp.maximum(chip - 1, 0)
    has_up = chip < nchip - 1
    has_down = chip >= 1
    partner = 2 * chip + (1 - core)
    plus_same, plus_other = 2 * up + core, 2 * up + (1 - core)
    minus_same, minus_other = 2 * down + core, 2 * down + (1 - core)
    upward = core == 1
    far_to = jnp.where(upward, plus_other, minus_other)
    far_from = jnp.where(upward, M_SAME, P_SAME)
    sends_far = has_up & has_down
    has_far = jnp.where(upward, chip < nchip - 2, chip >= 2)
    def stepped(place):
        return lax.rem(place + PLANE, PLANE) == 0

    spared_bins = jnp.where(upward, DETOURS, DETOURS_DOWN)
    spared = sends_far & jnp.where(upward, stepped(chip + 1), stepped(chip))
    detours = jnp.where(upward, stepped(chip + 3) & (chip + 4 < nchip), stepped(chip - 2) & (chip >= 4))
    relays = jnp.where(upward, stepped(chip - 1) & (chip >= 4), stepped(chip + 2) & (chip + 4 < nchip))
    four_up, four_down = 2 * jnp.minimum(chip + 4, nchip - 1) + core, 2 * jnp.maximum(chip - 4, 0) + core
    detour_to = jnp.where(upward, four_up, four_down)
    detour_from = jnp.where(upward, P_SAME, M_SAME)
    relay_from = jnp.where(upward, four_down, four_up)
    relay_to = jnp.where(upward, minus_other, plus_other)
    crosses = jnp.where(upward, stepped(chip + 2) & (chip + 3 < nchip), stepped(chip - 1) & (chip >= 3))
    cross_to = jnp.where(
        upward, 2 * jnp.minimum(chip + 3, nchip - 1), 2 * jnp.maximum(chip - 3, 0) + 1)
    crossed = sends_far & jnp.where(upward, stepped(chip), stepped(chip + 1))
    tells = jnp.where(upward, stepped(chip + 1) & has_up, stepped(chip) & has_down)
    told = jnp.where(upward, minus_same, plus_same)
    late_m = (lax.rem(chip, PLANE) == 0) & has_down
    late_p = (lax.rem(chip + 1, PLANE) == 0) & has_up
    edge = late_m | late_p
    p_early = lax.rem(chip, ROW) < 2

    def coded(units, field, bits):
        m_first, p_first, m, p = (packed([unit[field] for unit in order[units]], bits) for order in ORDERS)
        return jnp.where(late_m, m, jnp.where(late_p, p, jnp.where(p_early, p_first, m_first)))

    units = len(ORDERS[0])
    codes = [(coded(slice(n, None, 2), 0, 3), coded(slice(n, None, 2), 1, 2)) for n in range(2)]
    alone = coded(slice(units - ALONE, None), 0, 3), coded(slice(units - ALONE, None), 1, 2)
    singles = jnp.where(edge, 0, ALONE)
    pairs = (units - singles) // 2

    def unit_at(code, i):
        return (code[0] >> (3 * i)) & 7, (code[1] >> (2 * i)) & 3

    barrier = pltpu.get_barrier_semaphore()

    def greet(peer):
        pl.semaphore_signal(barrier, inc=1, device_id=(peer,), device_id_type=MESH)

    @pl.when(has_up)
    def _():
        greet(plus_same)
        greet(plus_other)

    @pl.when(has_down)
    def _():
        greet(minus_same)
        greet(minus_other)

    greet(partner)
    pl.when(detours)(lambda: greet(detour_to))
    pl.when(relays)(lambda: greet(relay_from))

    def own_load(f):
        return pltpu.make_async_copy(spec_ref.at[f], blk.at[OWN, f], local_sem.at[f])

    bins_load = pltpu.make_async_copy(bins_hbm, bins_ref, in_sem.at[0])
    off_load = pltpu.make_async_copy(off_ref, offs.at[OWN], in_sem.at[1])
    bins_load.start()
    off_load.start()
    for f in range(nfreq):
        own_load(f).start()

    def clear(slots, freqs):
        for slot in slots:
            offs[slot] = jnp.zeros(offs.shape[1:], offs.dtype)
            for f in range(freqs):
                blk[slot, f] = jnp.zeros(blk.shape[2:], blk.dtype)

    @pl.when(jnp.logical_not(has_down))
    def _():
        clear((M_SAME, M_OTHER), nfreq)

    @pl.when(jnp.logical_not(has_up))
    def _():
        clear((P_SAME, P_OTHER), nfreq)

    @pl.when(jnp.logical_not(has_far))
    def _():
        clear((FAR,), nfreq)

    aug[...] = jnp.zeros_like(aug)
    wre[:, lanes:, :] = jnp.zeros((nfreq, wre.shape[1] - lanes, nch), BF16)
    wim[:, lanes:, :] = jnp.zeros((nfreq, wim.shape[1] - lanes, nch), BF16)

    def send(kind, f, src, slot, to):
        return pltpu.make_async_remote_copy(
            src_ref=src, dst_ref=blk.at[slot, f], send_sem=send_sem.at[kind, f],
            recv_sem=recv_sem.at[slot, f], device_id=(to,), device_id_type=MESH)

    def to_plus(f):
        return send(TO_PLUS, f, blk.at[OWN, f], M_SAME, plus_same)

    def to_minus(f):
        return send(TO_MINUS, f, blk.at[OWN, f], P_SAME, minus_same)

    def to_partner(f):
        return send(TO_PARTNER, f, blk.at[OWN, f], PARTNER, partner)

    def forward(slot, f):
        return send(slot + FWD_M - M_SAME, f, blk.at[slot, f], slot + M_OTHER - M_SAME, partner)

    def forward_far(f):
        return send(FWD_FAR, f, blk.at[far_from, f], FAR, far_to)

    def detour(f):
        return pltpu.make_async_remote_copy(
            src_ref=blk.at[detour_from, f], dst_ref=via.at[f], send_sem=send_sem.at[DETOUR, f],
            recv_sem=via_recv.at[f], device_id=(detour_to,), device_id_type=MESH)

    def cross():
        return send(DETOUR, nfreq - 1, blk.at[detour_from, nfreq - 1], FAR, cross_to)

    def relay(f):
        return send(DETOUR, f, via.at[f], FAR, relay_to)

    def off_copy(n, src, slot, to):
        return pltpu.make_async_remote_copy(
            src_ref=src, dst_ref=offs.at[slot], send_sem=off_send.at[n],
            recv_sem=off_recv.at[slot], device_id=(to,), device_id_type=MESH)

    off_partner = off_copy(0, off_ref, PARTNER, partner)
    off_up = (off_copy(1, off_ref, M_SAME, plus_same), off_copy(3, off_ref, M_OTHER, plus_other))
    off_down = (off_copy(2, off_ref, P_SAME, minus_same), off_copy(4, off_ref, P_OTHER, minus_other))
    off_far = off_copy(5, offs.at[far_from], FAR, far_to)
    off_detour = pltpu.make_async_remote_copy(
        src_ref=offs.at[detour_from], dst_ref=via_off, send_sem=off_send.at[6],
        recv_sem=via_recv.at[DETOURS], device_id=(detour_to,), device_id_type=MESH)
    off_relay = off_copy(6, via_off, FAR, relay_to)

    def wait_block(slot, f):
        send(TO_PLUS, f, spec_ref.at[f], slot, partner).wait_recv()

    def wait_offsets(slot):
        off_copy(0, off_ref, slot, partner).wait_recv()

    row = lax.broadcasted_iota(jnp.int32, (8, lanes), 0)
    part = row & 3

    def pick(parts, a, b, c, d):
        return jnp.where(parts == 0, a, jnp.where(parts == 1, b, jnp.where(parts == 2, c, d)))

    def tables(off):
        shape = off.shape
        place = lax.broadcasted_iota(jnp.int32, shape, 1) * lanes + lax.broadcasted_iota(jnp.int32, shape, 2)
        pos = place * spacing_metres + off
        result = []
        for f in range(nfreq):
            cos, sin = cos_sin((bins_ref[f] * pos) & (period_metres - 1))
            result.append(split(cos) + split(sin))
        return result

    def put_aug(slot, table, n):
        for g in range(groups):
            rows = []
            for f in range(nfreq):
                ch, cl, sh, sl = (v[n, g : g + 1, :] for v in table[f])
                rows.append(pick(part, ch, cl, sh, sl))
            block = jnp.concatenate(rows, axis=0)
            aug[slot, g * lanes : (g + 1) * lanes, 0 : 8 * nfreq] = block.T.astype(BF16)

    bins_load.wait()
    off_load.wait()
    own_table = tables(offs[OWN : OWN + 1])
    put_aug(OWN, own_table, 0)
    late = row >= 4
    cosine = part < 2
    nothing = jnp.zeros((8, lanes), F32)
    for g in range(groups):
        for f in range(nfreq):
            ch, cl, sh, sl = (v[0, g : g + 1, :] for v in own_table[f])
            cos = jnp.where(late, cl, ch)
            sin = jnp.where(late, sl, sh)
            real = jnp.where(cosine, cos, sin) * (-model_amp)
            imag = jnp.where(cosine, sin, -cos) * model_amp
            cols = slice(g * lanes, (g + 1) * lanes)
            rows = slice(lanes, lanes + 8 * nfreq)
            wre[f, rows, cols] = jnp.concatenate(
                [real if n == f else nothing for n in range(nfreq)], axis=0).astype(BF16)
            wim[f, rows, cols] = jnp.concatenate(
                [imag if n == f else nothing for n in range(nfreq)], axis=0).astype(BF16)

    def open_links():
        greeted = 1 + 2 * has_up.astype(jnp.int32) + 2 * has_down.astype(jnp.int32)
        greeted += (detours | relays).astype(jnp.int32)
        pl.semaphore_wait(barrier, greeted)

        @pl.when(has_up)
        def _():
            to_plus(0).start()
            for copy in off_up:
                copy.start()

        @pl.when(has_down)
        def _():
            to_minus(0).start()
            for copy in off_down:
                copy.start()

        off_partner.start()
        to_partner(0).start()
        for f in range(1, nfreq):
            pl.when(has_up)(lambda f=f: to_plus(f).start())
            pl.when(has_down)(lambda f=f: to_minus(f).start())
            to_partner(f).start()

    for f in range(nfreq):
        own_load(f).wait()
    pl.when(jnp.logical_not(late_m))(open_links)

    half = lanes // 2
    scale = 1.0 / half

    def transposed(slot, f):
        t = blk[slot, f].T
        return t, jnp.concatenate([-t[half:], t[:half]], axis=0)

    def grads(slot, f):
        x = jnp.concatenate([blk[slot, f], aug[slot]], axis=1)
        real = jnp.tanh(dot(x, wre[f])).astype(BF16)
        imag = jnp.tanh(dot(x, wim[f])).astype(BF16)
        return real, imag

    def terms(slot, f, g):
        t, swapped = transposed(slot, f)
        return dot(t, g[0]) + dot(swapped, g[1])

    def own_step(i, carry):
        fs = [2 * i, 2 * i + 1]
        for f in fs:
            t, swapped = transposed(OWN, f)
            wre[f, :lanes, :] = t * jnp.array(scale, BF16)
            wim[f, :lanes, :] = swapped * jnp.array(-scale, BF16)
        g = [grads(OWN, f) for f in fs]
        for f, v in zip(fs, g):
            acc[f] = 2.0 * terms(OWN, f, v)
        return carry

    lax.fori_loop(0, nfreq // 2, own_step, 0)
    pl.when(late_m)(open_links)

    wait_offsets(PARTNER)
    put_aug(PARTNER, tables(offs[PARTNER : PARTNER + 1]), 0)

    def partner_step(i, carry):
        fs = [2 * i, 2 * i + 1]
        for f in fs:
            wait_block(PARTNER, f)
        g = [grads(PARTNER, f) for f in fs]
        for f, v in zip(fs, g):
            acc[f] += terms(PARTNER, f, v)
        return carry

    lax.fori_loop(0, nfreq // 2, partner_step, 0)

    @pl.when(has_down)
    def _():
        wait_offsets(M_SAME)
        wait_offsets(M_OTHER)

    @pl.when(has_up)
    def _():
        wait_offsets(P_SAME)
        wait_offsets(P_OTHER)

    @pl.when(sends_far & jnp.logical_not(spared))
    def _():
        off_far.start()

    pl.when(detours)(lambda: off_detour.start())

    table = tables(offs[M_SAME : P_OTHER + 1])
    for slot in range(M_SAME, P_OTHER + 1):
        put_aug(slot, table, slot - M_SAME)

    def arrive(slot, f):
        there = jnp.where(slot == FAR, has_far, jnp.where((slot & 1) == 1, has_up, has_down))

        @pl.when(there)
        def _():
            wait_block(slot, f)

        @pl.when(there & (slot <= P_SAME))
        def _():
            forward(slot, f).start()

        @pl.when(tells & (slot == detour_from) & (f == 0))
        def _():
            pl.semaphore_signal(token, inc=1, device_id=(told,), device_id_type=MESH)

        elsewhere = (spared & (f < spared_bins)) | (crossed & (f == nfreq - 1))

        @pl.when(sends_far & (slot == far_from) & jnp.logical_not(elsewhere))
        def _():
            forward_far(f).start()

        @pl.when((slot == FAR) & (f == 0))
        def _():
            pl.when(has_far)(lambda: wait_offsets(FAR))
            put_aug(FAR, tables(offs[FAR : FAR + 1]), 0)

    def deliver(slot, f):
        @pl.when(slot == FAR)
        def _():
            out_ref[f] = acc[f].T * scale

    def sent():
        off_partner.wait_send()

        @pl.when(has_up)
        def _():
            for copy in off_up:
                copy.wait_send()

        @pl.when(has_down)
        def _():
            for copy in off_down:
                copy.wait_send()

        pl.when(sends_far & jnp.logical_not(spared))(lambda: off_far.wait_send())
        pl.when(detours)(lambda: off_detour.wait_send())
        pl.when(relays)(lambda: off_relay.wait_send())
        for f in range(nfreq):
            to_partner(f).wait_send()
            pl.when(has_up)(lambda: to_plus(f).wait_send())
            pl.when(has_down)(lambda: to_minus(f).wait_send())

    def step(i, carry):
        (slot0, f0), (slot1, f1) = (unit_at(code, i) for code in codes)
        arrive(slot0, f0)
        arrive(slot1, f1)

        for n in range(DETOURS):
            pl.when((i == 2 * n) & detours & (n < spared_bins))(lambda n=n: detour(n).start())

        @pl.when((i == 2) & relays)
        def _():
            off_detour.wait_recv()
            off_relay.start()

        for n in range(DETOURS):
            @pl.when((i == 2 * n + 2) & relays & (n < spared_bins))
            def _():
                detour(n).wait_recv()
                relay(n).start()

        @pl.when((i == 2 * nfreq - 2) & crosses)
        def _():
            pl.semaphore_wait(token, 1)
            cross().start()

        g0 = grads(slot0, f0)
        g1 = grads(slot1, f1)
        acc[f0] += terms(slot0, f0, g0)
        acc[f1] += terms(slot1, f1, g1)
        deliver(slot0, f0)
        deliver(slot1, f1)
        return carry

    lax.fori_loop(0, pairs, step, 0)
    sent()

    def last_step(i, carry):
        slot, f = unit_at(alone, i)
        arrive(slot, f)
        acc[f] += terms(slot, f, grads(slot, f))
        deliver(slot, f)
        return carry

    lax.fori_loop(0, singles, last_step, 0)

    for f in range(nfreq):
        pl.when(has_up)(lambda: forward(P_SAME, f).wait_send())
        pl.when(has_down)(lambda: forward(M_SAME, f).wait_send())
        if f < DETOURS:
            pl.when(sends_far & jnp.logical_not(spared & (f < spared_bins)))(lambda: forward_far(f).wait_send())
            pl.when(detours & (f < spared_bins))(lambda: detour(f).wait_send())
            pl.when(relays & (f < spared_bins))(lambda: relay(f).wait_send())
        elif f < nfreq - 1:
            pl.when(sends_far)(lambda: forward_far(f).wait_send())
        else:
            pl.when(sends_far & jnp.logical_not(crossed))(lambda: forward_far(f).wait_send())
            pl.when(crosses)(lambda: cross().wait_send())


def local(ndev, spectra, offsets, bins):
    nfreq, nch, width = spectra.shape
    lanes = 128
    assert width == lanes and nch % lanes == 0 and nfreq % 2 == 0 and 8 * nfreq <= lanes
    assert (nch * spacing_metres) % period_metres == 0 and nfreq == 4
    hbm = pl.BlockSpec(memory_space=pltpu.HBM)
    args = (bins, offsets.reshape(nch // lanes, lanes), spectra)
    return pl.pallas_call(
        functools.partial(kernel, nfreq, nch, ndev),
        out_shape=jax.ShapeDtypeStruct((nfreq, nch, width), F32),
        in_specs=[hbm, hbm, hbm],
        out_specs=pl.BlockSpec(memory_space=pltpu.VMEM),
        scratch_shapes=[
            pltpu.VMEM((7, nfreq, nch, width), BF16),
            pltpu.VMEM((7, nch, lanes), BF16),
            pltpu.VMEM((nfreq, 2 * lanes, nch), BF16),
            pltpu.VMEM((nfreq, 2 * lanes, nch), BF16),
            pltpu.VMEM((nfreq, width, nch), F32),
            pltpu.VMEM((7, nch // lanes, lanes), jnp.int32),
            pltpu.SMEM((nfreq,), jnp.int32),
            pltpu.SemaphoreType.DMA((2,)),
            pltpu.SemaphoreType.DMA((nfreq,)),
            pltpu.SemaphoreType.DMA((7, nfreq)),
            pltpu.SemaphoreType.DMA((7, nfreq)),
            pltpu.SemaphoreType.DMA((7,)),
            pltpu.SemaphoreType.DMA((7,)),
            pltpu.VMEM((DETOURS, nch, width), BF16),
            pltpu.VMEM((nch // lanes, lanes), jnp.int32),
            pltpu.SemaphoreType.DMA((DETOURS + 1,)),
            pltpu.SemaphoreType.REGULAR,
        ],
        compiler_params=pltpu.CompilerParams(
            collective_id=0, has_side_effects=True, vmem_limit_bytes=24 << 20),
    )(*(pltpu.with_memory_space_constraint(v, pltpu.HBM) for v in args))


def solution(mesh):
    return jax.shard_map(
        functools.partial(local, mesh.shape["ch"]),
        mesh=mesh,
        in_specs=(P(None, "ch", None), P("ch"), P()),
        out_specs=P(None, "ch", None),
        check_vma=False,
    )
```

```python
import functools
import math

import jax
import jax.numpy as jnp
from jax import lax
from jax.experimental import pallas as pl
from jax.experimental.pallas import tpu as pltpu
from jax.sharding import PartitionSpec as P

spacing_metres = 8
period_metres = 4096
model_amp = 0.5

F32 = jnp.float32
BF16 = jnp.bfloat16
MESH = pl.DeviceIdType.MESH

OWN, PARTNER, M_SAME, P_SAME, M_OTHER, P_OTHER, FAR = range(7)
TO_PARTNER, TO_PLUS, TO_MINUS, FWD_M, FWD_P, FWD_FAR, DETOUR = range(7)

PLANE, ROW = 16, 4
DETOURS, DETOURS_DOWN = 1, 1
ALONE = 4

def even(one, one_other, two, two_other):
    near = sum(([(one, f), (two, f), (one_other, f), (two_other, f)] for f in range(4)), [])
    return near + [(FAR, f) for f in range(4)]


def lopsided(early, early_other, late, late_other):
    start = [
        (early, 0), (early, 1), (early_other, 0), (early_other, 1), (early, 2), (late, 0), (early_other, 2),
        (late_other, 0), (early, 3), (late, 1), (early_other, 3), (late_other, 1)]
    return start + [
        (late, 2), (FAR, 0), (late_other, 2), (late, 3), (late_other, 3), (FAR, 1), (FAR, 2), (FAR, 3)]


M_FIRST, P_FIRST = (M_SAME, M_OTHER, P_SAME, P_OTHER), (P_SAME, P_OTHER, M_SAME, M_OTHER)
ORDERS = (even(*M_FIRST), even(*P_FIRST), lopsided(*P_FIRST), lopsided(*M_FIRST))


def packed(values, bits):
    return sum(v << (bits * i) for i, v in enumerate(values))


def dot(a, b):
    return lax.dot_general(a, b, (((1,), (0,)), ((), ())), preferred_element_type=F32)


def cos_sin(m):
    quarter = period_metres // 4
    turn = (m + quarter // 2) // quarter
    theta = (m - turn * quarter).astype(F32) * (2.0 * math.pi / period_metres)
    x = theta * theta
    s = theta * (1.0 + x * (-1.0 / 6 + x * (1.0 / 120 + x * (-1.0 / 5040 + x * (1.0 / 362880)))))
    c = 1.0 + x * (-0.5 + x * (1.0 / 24 + x * (-1.0 / 720 + x * (1.0 / 40320))))
    turn = turn & 3
    odd = (turn & 1) == 1
    cos = jnp.where(odd, s, c)
    sin = jnp.where(odd, c, s)
    cos = jnp.where((turn == 1) | (turn == 2), -cos, cos)
    sin = jnp.where(turn >= 2, -sin, sin)
    return cos, sin


def split(v):
    high = v.astype(BF16).astype(F32)
    return high, v - high


def kernel(nfreq, nch, ndev, bins_hbm, off_ref, spec_ref, out_ref, blk, aug, wre, wim, acc, offs, bins_ref,
           in_sem, local_sem, send_sem, recv_sem, off_send, off_recv, via, via_off, via_recv, token):
    lanes = 128
    groups = nch // lanes
    me = lax.axis_index("ch")
    nchip = ndev // 2
    chip = me // 2
    core = me - 2 * chip
    up = jnp.minimum(chip + 1, nchip - 1)
    down = jnp.maximum(chip - 1, 0)
    has_up = chip < nchip - 1
    has_down = chip >= 1
    partner = 2 * chip + (1 - core)
    plus_same, plus_other = 2 * up + core, 2 * up + (1 - core)
    minus_same, minus_other = 2 * down + core, 2 * down + (1 - core)
    upward = core == 1
    far_to = jnp.where(upward, plus_other, minus_other)
    far_from = jnp.where(upward, M_SAME, P_SAME)
    sends_far = has_up & has_down
    has_far = jnp.where(upward, chip < nchip - 2, chip >= 2)
    def stepped(place):
        return lax.rem(place + PLANE, PLANE) == 0

    spared_bins = jnp.where(upward, DETOURS, DETOURS_DOWN)
    spared = sends_far & jnp.where(upward, stepped(chip + 1), stepped(chip))
    detours = jnp.where(upward, stepped(chip + 3) & (chip + 4 < nchip), stepped(chip - 2) & (chip >= 4))
    relays = jnp.where(upward, stepped(chip - 1) & (chip >= 4), stepped(chip + 2) & (chip + 4 < nchip))
    four_up, four_down = 2 * jnp.minimum(chip + 4, nchip - 1) + core, 2 * jnp.maximum(chip - 4, 0) + core
    detour_to = jnp.where(upward, four_up, four_down)
    detour_from = jnp.where(upward, P_SAME, M_SAME)
    relay_from = jnp.where(upward, four_down, four_up)
    relay_to = jnp.where(upward, minus_other, plus_other)
    crosses = jnp.where(upward, stepped(chip + 2) & (chip + 3 < nchip), stepped(chip - 1) & (chip >= 3))
    cross_to = jnp.where(
        upward, 2 * jnp.minimum(chip + 3, nchip - 1), 2 * jnp.maximum(chip - 3, 0) + 1)
    crossed = sends_far & jnp.where(upward, stepped(chip), stepped(chip + 1))
    tells = jnp.where(upward, stepped(chip + 1) & has_up, stepped(chip) & has_down)
    told = jnp.where(upward, minus_same, plus_same)
    late_m = (lax.rem(chip, PLANE) == 0) & has_down
    late_p = (lax.rem(chip + 1, PLANE) == 0) & has_up
    edge = late_m | late_p
    p_early = lax.rem(chip, ROW) < 2

    def coded(units, field, bits):
        m_first, p_first, m, p = (packed([unit[field] for unit in order[units]], bits) for order in ORDERS)
        return jnp.where(late_m, m, jnp.where(late_p, p, jnp.where(p_early, p_first, m_first)))

    units = len(ORDERS[0])
    codes = [(coded(slice(n, None, 2), 0, 3), coded(slice(n, None, 2), 1, 2)) for n in range(2)]
    alone = coded(slice(units - ALONE, None), 0, 3), coded(slice(units - ALONE, None), 1, 2)
    singles = jnp.where(edge, ALONE // 2, ALONE)
    pairs = (units - singles) // 2

    def unit_at(code, i):
        return (code[0] >> (3 * i)) & 7, (code[1] >> (2 * i)) & 3

    barrier = pltpu.get_barrier_semaphore()

    def greet(peer):
        pl.semaphore_signal(barrier, inc=1, device_id=(peer,), device_id_type=MESH)

    @pl.when(has_up)
    def _():
        greet(plus_same)
        greet(plus_other)

    @pl.when(has_down)
    def _():
        greet(minus_same)
        greet(minus_other)

    greet(partner)
    pl.when(detours)(lambda: greet(detour_to))
    pl.when(relays)(lambda: greet(relay_from))

    def own_load(f):
        return pltpu.make_async_copy(spec_ref.at[f], blk.at[OWN, f], local_sem.at[f])

    bins_load = pltpu.make_async_copy(bins_hbm, bins_ref, in_sem.at[0])
    off_load = pltpu.make_async_copy(off_ref, offs.at[OWN], in_sem.at[1])
    bins_load.start()
    off_load.start()
    for f in range(nfreq):
        own_load(f).start()

    def clear(slots, freqs):
        for slot in slots:
            offs[slot] = jnp.zeros(offs.shape[1:], offs.dtype)
            for f in range(freqs):
                blk[slot, f] = jnp.zeros(blk.shape[2:], blk.dtype)

    @pl.when(jnp.logical_not(has_down))
    def _():
        clear((M_SAME, M_OTHER), nfreq)

    @pl.when(jnp.logical_not(has_up))
    def _():
        clear((P_SAME, P_OTHER), nfreq)

    @pl.when(jnp.logical_not(has_far))
    def _():
        clear((FAR,), nfreq)

    aug[...] = jnp.zeros_like(aug)
    wre[:, lanes:, :] = jnp.zeros((nfreq, wre.shape[1] - lanes, nch), BF16)
    wim[:, lanes:, :] = jnp.zeros((nfreq, wim.shape[1] - lanes, nch), BF16)

    def send(kind, f, src, slot, to):
        return pltpu.make_async_remote_copy(
            src_ref=src, dst_ref=blk.at[slot, f], send_sem=send_sem.at[kind, f],
            recv_sem=recv_sem.at[slot, f], device_id=(to,), device_id_type=MESH)

    def to_plus(f):
        return send(TO_PLUS, f, blk.at[OWN, f], M_SAME, plus_same)

    def to_minus(f):
        return send(TO_MINUS, f, blk.at[OWN, f], P_SAME, minus_same)

    def to_partner(f):
        return send(TO_PARTNER, f, blk.at[OWN, f], PARTNER, partner)

    def forward(slot, f):
        return send(slot + FWD_M - M_SAME, f, blk.at[slot, f], slot + M_OTHER - M_SAME, partner)

    def forward_far(f):
        return send(FWD_FAR, f, blk.at[far_from, f], FAR, far_to)

    def detour(f):
        return pltpu.make_async_remote_copy(
            src_ref=blk.at[detour_from, f], dst_ref=via.at[f], send_sem=send_sem.at[DETOUR, f],
            recv_sem=via_recv.at[f], device_id=(detour_to,), device_id_type=MESH)

    def cross():
        return send(DETOUR, nfreq - 1, blk.at[detour_from, nfreq - 1], FAR, cross_to)

    def relay(f):
        return send(DETOUR, f, via.at[f], FAR, relay_to)

    def off_copy(n, src, slot, to):
        return pltpu.make_async_remote_copy(
            src_ref=src, dst_ref=offs.at[slot], send_sem=off_send.at[n],
            recv_sem=off_recv.at[slot], device_id=(to,), device_id_type=MESH)

    off_partner = off_copy(0, off_ref, PARTNER, partner)
    off_up = (off_copy(1, off_ref, M_SAME, plus_same), off_copy(3, off_ref, M_OTHER, plus_other))
    off_down = (off_copy(2, off_ref, P_SAME, minus_same), off_copy(4, off_ref, P_OTHER, minus_other))
    off_far = off_copy(5, offs.at[far_from], FAR, far_to)
    off_detour = pltpu.make_async_remote_copy(
        src_ref=offs.at[detour_from], dst_ref=via_off, send_sem=off_send.at[6],
        recv_sem=via_recv.at[DETOURS], device_id=(detour_to,), device_id_type=MESH)
    off_relay = off_copy(6, via_off, FAR, relay_to)

    def wait_block(slot, f):
        send(TO_PLUS, f, spec_ref.at[f], slot, partner).wait_recv()

    def wait_offsets(slot):
        off_copy(0, off_ref, slot, partner).wait_recv()

    row = lax.broadcasted_iota(jnp.int32, (8, lanes), 0)
    part = row & 3

    def pick(parts, a, b, c, d):
        return jnp.where(parts == 0, a, jnp.where(parts == 1, b, jnp.where(parts == 2, c, d)))

    def tables(off):
        shape = off.shape
        place = lax.broadcasted_iota(jnp.int32, shape, 1) * lanes + lax.broadcasted_iota(jnp.int32, shape, 2)
        pos = place * spacing_metres + off
        result = []
        for f in range(nfreq):
            cos, sin = cos_sin((bins_ref[f] * pos) & (period_metres - 1))
            result.append(split(cos) + split(sin))
        return result

    def put_aug(slot, table, n):
        for g in range(groups):
            rows = []
            for f in range(nfreq):
                ch, cl, sh, sl = (v[n, g : g + 1, :] for v in table[f])
                rows.append(pick(part, ch, cl, sh, sl))
            block = jnp.concatenate(rows, axis=0)
            aug[slot, g * lanes : (g + 1) * lanes, 0 : 8 * nfreq] = block.T.astype(BF16)

    bins_load.wait()
    off_load.wait()
    own_table = tables(offs[OWN : OWN + 1])
    put_aug(OWN, own_table, 0)
    late = row >= 4
    cosine = part < 2
    nothing = jnp.zeros((8, lanes), F32)
    for g in range(groups):
        for f in range(nfreq):
            ch, cl, sh, sl = (v[0, g : g + 1, :] for v in own_table[f])
            cos = jnp.where(late, cl, ch)
            sin = jnp.where(late, sl, sh)
            real = jnp.where(cosine, cos, sin) * (-model_amp)
            imag = jnp.where(cosine, sin, -cos) * model_amp
            cols = slice(g * lanes, (g + 1) * lanes)
            rows = slice(lanes, lanes + 8 * nfreq)
            wre[f, rows, cols] = jnp.concatenate(
                [real if n == f else nothing for n in range(nfreq)], axis=0).astype(BF16)
            wim[f, rows, cols] = jnp.concatenate(
                [imag if n == f else nothing for n in range(nfreq)], axis=0).astype(BF16)

    def open_links():
        greeted = 1 + 2 * has_up.astype(jnp.int32) + 2 * has_down.astype(jnp.int32)
        greeted += (detours | relays).astype(jnp.int32)
        pl.semaphore_wait(barrier, greeted)

        @pl.when(has_up)
        def _():
            to_plus(0).start()
            for copy in off_up:
                copy.start()

        @pl.when(has_down)
        def _():
            to_minus(0).start()
            for copy in off_down:
                copy.start()

        off_partner.start()
        to_partner(0).start()
        for f in range(1, nfreq):
            pl.when(has_up)(lambda f=f: to_plus(f).start())
            pl.when(has_down)(lambda f=f: to_minus(f).start())
            to_partner(f).start()

    for f in range(nfreq):
        own_load(f).wait()
    pl.when(jnp.logical_not(late_m))(open_links)

    half = lanes // 2
    scale = 1.0 / half

    def transposed(slot, f):
        t = blk[slot, f].T
        return t, jnp.concatenate([-t[half:], t[:half]], axis=0)

    def grads(slot, f):
        x = jnp.concatenate([blk[slot, f], aug[slot]], axis=1)
        real = jnp.tanh(dot(x, wre[f])).astype(BF16)
        imag = jnp.tanh(dot(x, wim[f])).astype(BF16)
        return real, imag

    def terms(slot, f, g):
        t, swapped = transposed(slot, f)
        return dot(t, g[0]) + dot(swapped, g[1])

    def own_step(i, carry):
        fs = [2 * i, 2 * i + 1]
        for f in fs:
            t, swapped = transposed(OWN, f)
            wre[f, :lanes, :] = t * jnp.array(scale, BF16)
            wim[f, :lanes, :] = swapped * jnp.array(-scale, BF16)
        g = [grads(OWN, f) for f in fs]
        for f, v in zip(fs, g):
            acc[f] = 2.0 * terms(OWN, f, v)
        return carry

    lax.fori_loop(0, nfreq // 2, own_step, 0)
    pl.when(late_m)(open_links)

    wait_offsets(PARTNER)
    put_aug(PARTNER, tables(offs[PARTNER : PARTNER + 1]), 0)

    def partner_step(i, carry):
        fs = [2 * i, 2 * i + 1]
        for f in fs:
            wait_block(PARTNER, f)
        g = [grads(PARTNER, f) for f in fs]
        for f, v in zip(fs, g):
            acc[f] += terms(PARTNER, f, v)
        return carry

    lax.fori_loop(0, nfreq // 2, partner_step, 0)

    @pl.when(has_down)
    def _():
        wait_offsets(M_SAME)
        wait_offsets(M_OTHER)

    @pl.when(has_up)
    def _():
        wait_offsets(P_SAME)
        wait_offsets(P_OTHER)

    @pl.when(sends_far & jnp.logical_not(spared))
    def _():
        off_far.start()

    pl.when(detours)(lambda: off_detour.start())

    table = tables(offs[M_SAME : P_OTHER + 1])
    for slot in range(M_SAME, P_OTHER + 1):
        put_aug(slot, table, slot - M_SAME)

    def arrive(slot, f):
        there = jnp.where(slot == FAR, has_far, jnp.where((slot & 1) == 1, has_up, has_down))

        @pl.when(there)
        def _():
            wait_block(slot, f)

        @pl.when(there & (slot <= P_SAME))
        def _():
            forward(slot, f).start()

        @pl.when(tells & (slot == detour_from) & (f == 0))
        def _():
            pl.semaphore_signal(token, inc=1, device_id=(told,), device_id_type=MESH)

        elsewhere = (spared & (f < spared_bins)) | (crossed & (f == nfreq - 1))

        @pl.when(sends_far & (slot == far_from) & jnp.logical_not(elsewhere))
        def _():
            forward_far(f).start()

        @pl.when((slot == FAR) & (f == 0))
        def _():
            pl.when(has_far)(lambda: wait_offsets(FAR))
            put_aug(FAR, tables(offs[FAR : FAR + 1]), 0)

    def deliver(slot, f):
        @pl.when(slot == FAR)
        def _():
            out_ref[f] = acc[f].T * scale

    def sent():
        off_partner.wait_send()

        @pl.when(has_up)
        def _():
            for copy in off_up:
                copy.wait_send()

        @pl.when(has_down)
        def _():
            for copy in off_down:
                copy.wait_send()

        pl.when(sends_far & jnp.logical_not(spared))(lambda: off_far.wait_send())
        pl.when(detours)(lambda: off_detour.wait_send())
        pl.when(relays)(lambda: off_relay.wait_send())
        for f in range(nfreq):
            to_partner(f).wait_send()
            pl.when(has_up)(lambda: to_plus(f).wait_send())
            pl.when(has_down)(lambda: to_minus(f).wait_send())

    def step(i, carry):
        (slot0, f0), (slot1, f1) = (unit_at(code, i) for code in codes)
        arrive(slot0, f0)
        arrive(slot1, f1)

        for n in range(DETOURS):
            pl.when((i == 2 * n) & detours & (n < spared_bins))(lambda n=n: detour(n).start())

        @pl.when((i == 2) & relays)
        def _():
            off_detour.wait_recv()
            off_relay.start()

        for n in range(DETOURS):
            @pl.when((i == 2 * n + 2) & relays & (n < spared_bins))
            def _():
                detour(n).wait_recv()
                relay(n).start()

        @pl.when((i == 2 * nfreq - 2) & crosses)
        def _():
            pl.semaphore_wait(token, 1)
            cross().start()

        g0 = grads(slot0, f0)
        g1 = grads(slot1, f1)
        acc[f0] += terms(slot0, f0, g0)
        acc[f1] += terms(slot1, f1, g1)
        deliver(slot0, f0)
        deliver(slot1, f1)
        return carry

    lax.fori_loop(0, pairs, step, 0)
    sent()

    def last_step(i, carry):
        slot, f = unit_at(alone, i)
        arrive(slot, f)
        acc[f] += terms(slot, f, grads(slot, f))
        deliver(slot, f)
        return carry

    lax.fori_loop(ALONE - singles, ALONE, last_step, 0)

    for f in range(nfreq):
        pl.when(has_up)(lambda: forward(P_SAME, f).wait_send())
        pl.when(has_down)(lambda: forward(M_SAME, f).wait_send())
        if f < DETOURS:
            pl.when(sends_far & jnp.logical_not(spared & (f < spared_bins)))(lambda: forward_far(f).wait_send())
            pl.when(detours & (f < spared_bins))(lambda: detour(f).wait_send())
            pl.when(relays & (f < spared_bins))(lambda: relay(f).wait_send())
        elif f < nfreq - 1:
            pl.when(sends_far)(lambda: forward_far(f).wait_send())
        else:
            pl.when(sends_far & jnp.logical_not(crossed))(lambda: forward_far(f).wait_send())
            pl.when(crosses)(lambda: cross().wait_send())


def local(ndev, spectra, offsets, bins):
    nfreq, nch, width = spectra.shape
    lanes = 128
    assert width == lanes and nch % lanes == 0 and nfreq % 2 == 0 and 8 * nfreq <= lanes
    assert (nch * spacing_metres) % period_metres == 0 and nfreq == 4
    hbm = pl.BlockSpec(memory_space=pltpu.HBM)
    args = (bins, offsets.reshape(nch // lanes, lanes), spectra)
    return pl.pallas_call(
        functools.partial(kernel, nfreq, nch, ndev),
        out_shape=jax.ShapeDtypeStruct((nfreq, nch, width), F32),
        in_specs=[hbm, hbm, hbm],
        out_specs=pl.BlockSpec(memory_space=pltpu.VMEM),
        scratch_shapes=[
            pltpu.VMEM((7, nfreq, nch, width), BF16),
            pltpu.VMEM((7, nch, lanes), BF16),
            pltpu.VMEM((nfreq, 2 * lanes, nch), BF16),
            pltpu.VMEM((nfreq, 2 * lanes, nch), BF16),
            pltpu.VMEM((nfreq, width, nch), F32),
            pltpu.VMEM((7, nch // lanes, lanes), jnp.int32),
            pltpu.SMEM((nfreq,), jnp.int32),
            pltpu.SemaphoreType.DMA((2,)),
            pltpu.SemaphoreType.DMA((nfreq,)),
            pltpu.SemaphoreType.DMA((7, nfreq)),
            pltpu.SemaphoreType.DMA((7, nfreq)),
            pltpu.SemaphoreType.DMA((7,)),
            pltpu.SemaphoreType.DMA((7,)),
            pltpu.VMEM((DETOURS, nch, width), BF16),
            pltpu.VMEM((nch // lanes, lanes), jnp.int32),
            pltpu.SemaphoreType.DMA((DETOURS + 1,)),
            pltpu.SemaphoreType.REGULAR,
        ],
        compiler_params=pltpu.CompilerParams(
            collective_id=0, has_side_effects=True, vmem_limit_bytes=24 << 20),
    )(*(pltpu.with_memory_space_constraint(v, pltpu.HBM) for v in args))


def solution(mesh):
    return jax.shard_map(
        functools.partial(local, mesh.shape["ch"]),
        mesh=mesh,
        in_specs=(P(None, "ch", None), P("ch"), P()),
        out_specs=P(None, "ch", None),
        check_vma=False,
    )
```
